32 devices in a mesh: member: 4 (over x, core), tile: 8 (over z, y).
Axes of the slice: x: 2, y: 2, z: 4, core: 2. Of those that a mesh axis runs over, the one named last changes fastest.
Arguments:
- state: bfloat16 [4, 8, 32, 32, 384], P('member', 'tile'), may hold values from -6 to 6
- cotangent: bfloat16 [4, 8, 32, 32, 384], P('member', 'tile'), may hold values from -6 to 6
- neighbors: int32 [8, 8], replicated, may hold values from -1 to 7, as said below
- kernel: float32 [7, 7, 384], replicated, may hold values from -0.875 to 0.875
- conv_bias: float32 [384], replicated, may hold values from -3 to 3
- norm_gain: float32 [384], replicated, may hold values from 0.25 to 1.75
- norm_shift: float32 [384], replicated, may hold values from -2 to 2
- w_in: bfloat16 [384, 1536], replicated, may hold values from -0.3125 to 0.3125
- bias_in: float32 [1536], replicated, may hold values from -3 to 3
- w_out: bfloat16 [1536, 384], replicated, may hold values from -0.15625 to 0.15625
- bias_out: float32 [384], replicated, may hold values from -3 to 3
- layer_scale: float32 [384], replicated, may hold values from 0.3 to 1
Outputs:
- new_state: bfloat16 [4, 8, 32, 32, 384], P('member', 'tile')
- state_grad: bfloat16 [4, 8, 32, 32, 384], P('member', 'tile')
- grad_w_in: float32 [384, 1536], P(None, 'tile')
- grad_w_out: float32 [1536, 384], P('tile')
- grad_kernel: float32 [7, 7, 384], replicated
- grad_bias_in: float32 [1536], replicated
- grad_channels: float32 [5, 384], replicated
The draws below stay inside these ranges and needn't reach their ends.
Inputs may be any that keep to these rules, and one draw needn't show every extreme that they name: Land tiles and tiles beyond the band's northern or southern edge are -1; longitude wraps around over 6 columns. If neighbors[t, d] = s then neighbors[s, opposite of d] = t. Wet tiles are numbered column by column, the columns of 2 tiles taken alternately upward and downward, so two neighbouring wet tiles differ in index by at most 3, counted cyclically over all wet tiles.
All inputs are finite; a program needn't handle non-finite values.
Results may differ from the reference program's by a relative error of at most 0.0062.
Values may be sent and summed in bfloat16 or wider, within the bound.
A program may use at most 128 MiB of HBM per device.

```python
import math
import jax
import jax.numpy as jnp
from jax import lax

C = 384
HID = 1536
KS = 7
TS = 32
GRID_Y = 2
GRID_X = 6
TILES = 8
MEMBERS = 4
N_TILE = 8


def draw_neighbors(key, part):
    cells = GRID_X * GRID_Y
    order = jax.random.permutation(key, cells - 2)
    wet_at = jnp.zeros((cells,), jnp.int32).at[order[:N_TILE - 2]].set(1)
    wet_at = wet_at.at[cells - 2].set(1).at[cells - 1].set(1)
    place = jnp.arange(cells, dtype=jnp.int32)
    column = place // GRID_Y
    within = place % GRID_Y
    row = jnp.where(column % 2 == 0, within, GRID_Y - 1 - within)
    cell_at = row * GRID_X + column
    rank = (jnp.cumsum(wet_at) - 1).astype(jnp.int32)
    index_of = jnp.full((cells,), -1, jnp.int32).at[cell_at].set(jnp.where(wet_at > 0, rank, -1))
    slot = jnp.where(wet_at > 0, rank, N_TILE)
    tile_cell = jnp.zeros((N_TILE,), jnp.int32).at[slot].set(cell_at, mode='drop')
    tile_x = tile_cell % GRID_X
    tile_y = tile_cell // GRID_X
    steps_x = jnp.array([0, 0, 1, -1, 1, -1, 1, -1], jnp.int32)
    steps_y = jnp.array([1, -1, 0, 0, 1, 1, -1, -1], jnp.int32)
    next_x = (tile_x[:, None] + steps_x[None, :]) % GRID_X
    next_y = tile_y[:, None] + steps_y[None, :]
    inside = (next_y >= 0) & (next_y < GRID_Y)
    looked = index_of[jnp.clip(next_y, 0, GRID_Y - 1) * GRID_X + next_x]
    return jnp.where(inside, looked, -1).astype(jnp.int32)


def block_scale(rng, dims, split, least, largest):
    loudness = 1.0
    for position, shards_of in split:
        heights = jax.random.uniform(jax.random.fold_in(jax.random.fold_in(rng, 6), position), (shards_of,), jnp.float32, least / len(split), largest / len(split))
        loudness = loudness * jnp.repeat(jnp.exp(heights), dims[position] // shards_of).reshape((-1,) + (1,) * (len(dims) - 1 - position))
    return loudness


def bell_draw(own_key, dims, scale, reach, shards=(), kind=jnp.bfloat16):
    drawn = scale * jax.random.normal(own_key, dims, jnp.float32)
    if shards:
        drawn = drawn * block_scale(own_key, dims, shards, -0.22, 0.18)
    return jnp.clip(drawn, -reach, reach).astype(kind)


def setup_inputs(seed: int = 0) -> dict:
    arg_keys = jax.random.split(jax.random.key(seed), 13)
    return {
        "state": bell_draw(arg_keys[0], (MEMBERS, TILES, TS, TS, C), 1.0, 6.0, ((0, 4), (1, 8))),
        "cotangent": bell_draw(arg_keys[1], (MEMBERS, TILES, TS, TS, C), 1.0, 6.0, ((0, 4), (1, 8))),
        "neighbors": draw_neighbors(jax.random.fold_in(arg_keys[12], 71), 0),
        "kernel": bell_draw(arg_keys[3], (KS, KS, C), (KS * KS) ** -0.5, 0.875, (), jnp.float32),
        "conv_bias": bell_draw(arg_keys[4], (C,), 0.5, 3.0, (), jnp.float32),
        "norm_gain": jnp.clip(1.0 + 0.15 * jax.random.normal(arg_keys[5], (C,), jnp.float32), 0.25, 1.75),
        "norm_shift": bell_draw(arg_keys[6], (C,), 0.3, 2.0, (), jnp.float32),
        "w_in": bell_draw(arg_keys[7], (C, HID), C ** -0.5, 0.3125),
        "bias_in": bell_draw(arg_keys[8], (HID,), 0.5, 3.0, (), jnp.float32),
        "w_out": bell_draw(arg_keys[9], (HID, C), HID ** -0.5, 0.15625),
        "bias_out": bell_draw(arg_keys[10], (C,), 0.5, 3.0, (), jnp.float32),
        "layer_scale": jnp.clip(jnp.exp(jax.random.uniform(arg_keys[11], (C,), jnp.float32, math.log(0.3), math.log(1.0))), 0.3, 1.0),
    }


GELU_SCALE = 0.7978845608028654
GELU_CUBIC = 0.044715
EPSILON = 1e-06

def contract_rows(left, right):
    return lax.dot_general(left, right, (((0,), (0,)), ((), ())), preferred_element_type=jnp.float32)

def contract_cols(left, right):
    return lax.dot_general(left, right, (((1,), (1,)), ((), ())), preferred_element_type=jnp.float32)

def framed(center, north, south, east, west, north_east, north_west, south_east, south_west):
    lower = jnp.concatenate([south_west, south, south_east], axis=1)
    middle = jnp.concatenate([west, center, east], axis=1)
    upper = jnp.concatenate([north_west, north, north_east], axis=1)
    return jnp.concatenate([lower, middle, upper], axis=0)

def fetch(tiles, index):
    tile = tiles[jnp.maximum(index, 0)]
    return jnp.where(index >= 0, tile, jnp.zeros_like(tile))

def frame_from(tiles, links, center, margin):
    side = center.shape[0]
    edge = side - margin
    got = [fetch(tiles, links[way]) for way in range(8)]
    return framed(center, got[0][:margin], got[1][edge:], got[2][:, :margin], got[3][:, edge:], got[4][:margin, :margin], got[5][:margin, edge:], got[6][edge:, :margin], got[7][edge:, edge:])

def depthwise(padded, kernel):
    taps = kernel.shape[0]
    side = padded.shape[0] - taps + 1
    total = jnp.zeros((side, side, padded.shape[2]), jnp.float32)
    for row_off in range(taps):
        for col_off in range(taps):
            total = total + kernel[row_off, col_off] * padded[row_off:row_off + side, col_off:col_off + side].astype(jnp.float32)
    return total

def transposed(padded, kernel):
    taps = kernel.shape[0]
    side = padded.shape[0] - taps + 1
    total = jnp.zeros((side, side, padded.shape[2]), jnp.float32)
    for row_off in range(taps):
        for col_off in range(taps):
            row_at = taps - 1 - row_off
            col_at = taps - 1 - col_off
            total = total + kernel[row_off, col_off] * padded[row_at:row_at + side, col_at:col_at + side].astype(jnp.float32)
    return total

def kernel_grad(padded, grad_mixed):
    taps = padded.shape[0] - grad_mixed.shape[0] + 1
    side = grad_mixed.shape[0]
    rows = []
    for row_off in range(taps):
        line = []
        for col_off in range(taps):
            window = padded[row_off:row_off + side, col_off:col_off + side].astype(jnp.float32)
            line.append(lax.optimization_barrier(jnp.sum(window * grad_mixed, axis=(0, 1))))
        rows.append(jnp.stack(line))
    return jnp.stack(rows)

def forward_backward(padded, center, cot_tile, kernel, conv_bias, norm_gain, norm_shift, w_in, bias_in, w_out, bias_out, layer_scale):
    side, width = (center.shape[0], center.shape[2])
    mixed = (depthwise(padded, kernel) + conv_bias).reshape(side * side, width)
    centered = mixed - lax.optimization_barrier(jnp.mean(mixed, axis=1, keepdims=True))
    variance = lax.optimization_barrier(jnp.mean(centered * centered, axis=1, keepdims=True))
    inv_std = lax.rsqrt(variance + EPSILON)
    norm_hat = centered * inv_std
    normed = (norm_hat * norm_gain + norm_shift).astype(jnp.bfloat16)
    pre_act = jnp.dot(normed, w_in, preferred_element_type=jnp.float32) + bias_in
    tanh_value = jnp.tanh(GELU_SCALE * (pre_act + GELU_CUBIC * pre_act * pre_act * pre_act))
    activation = (0.5 * pre_act * (1.0 + tanh_value)).astype(jnp.bfloat16)
    branch = jnp.dot(activation, w_out, preferred_element_type=jnp.float32) + bias_out
    flat_state = center.reshape(side * side, width).astype(jnp.float32)
    new_tile = (flat_state + layer_scale * branch).astype(jnp.bfloat16).reshape(side, side, width)
    flat_cot = cot_tile.reshape(side * side, width).astype(jnp.float32)
    grad_branch = layer_scale * flat_cot
    branch_low = grad_branch.astype(jnp.bfloat16)
    grad_wout = contract_rows(activation, branch_low)
    grad_bout = lax.optimization_barrier(jnp.sum(grad_branch, axis=0))
    grad_gamma = lax.optimization_barrier(jnp.sum(flat_cot * branch, axis=0))
    grad_act = contract_cols(branch_low, w_out)
    slope = 0.5 * (1.0 + tanh_value) + 0.5 * pre_act * (1.0 - tanh_value * tanh_value) * GELU_SCALE * (1.0 + 3.0 * GELU_CUBIC * pre_act * pre_act)
    grad_pre = grad_act * slope
    grad_pre_b = grad_pre.astype(jnp.bfloat16)
    grad_win = contract_rows(normed, grad_pre_b)
    grad_bin = lax.optimization_barrier(jnp.sum(grad_pre, axis=0))
    grad_normed = contract_cols(grad_pre_b, w_in)
    grad_gain = lax.optimization_barrier(jnp.sum(grad_normed * norm_hat, axis=0))
    grad_shift = lax.optimization_barrier(jnp.sum(grad_normed, axis=0))
    scaled = grad_normed * norm_gain
    grad_mixed = inv_std * (scaled - lax.optimization_barrier(jnp.mean(scaled, axis=1, keepdims=True)) - norm_hat * lax.optimization_barrier(jnp.mean(scaled * norm_hat, axis=1, keepdims=True)))
    grad_mixed = grad_mixed.reshape(side, side, width)
    grad_kern = kernel_grad(padded, grad_mixed)
    grad_conv = lax.optimization_barrier(jnp.sum(grad_mixed, axis=(0, 1)))
    grads = (grad_win, grad_wout, grad_kern, grad_bin, grad_conv, grad_gain, grad_shift, grad_bout, grad_gamma)
    return (new_tile, grad_mixed.astype(jnp.bfloat16), grads)

def reference(state, cotangent, neighbors, kernel, conv_bias, norm_gain, norm_shift, w_in, bias_in, w_out, bias_out, layer_scale):
    members, count, side, width = (state.shape[0], state.shape[1], state.shape[2], state.shape[4])
    hidden = w_in.shape[1]
    taps = kernel.shape[0]
    margin = taps // 2

    def first(totals, index):
        member = index // count
        tile = index % count
        tiles = state[member]
        center = tiles[tile]
        padded = frame_from(tiles, neighbors[tile], center, margin)
        new_tile, grad_low, grads = forward_backward(padded, center, cotangent[member, tile], kernel, conv_bias, norm_gain, norm_shift, w_in, bias_in, w_out, bias_out, layer_scale)
        totals = tuple((total + term for total, term in zip(totals, grads)))
        return (totals, (new_tile, grad_low))
    zeros_c = jnp.zeros((width,), jnp.float32)
    start = (jnp.zeros((width, hidden), jnp.float32), jnp.zeros((hidden, width), jnp.float32), jnp.zeros((taps, taps, width), jnp.float32), jnp.zeros((hidden,), jnp.float32), zeros_c, zeros_c, zeros_c, zeros_c, zeros_c)
    totals, (news, grad_lows) = lax.scan(first, start, jnp.arange(members * count, dtype=jnp.int32))
    grad_lows = grad_lows.reshape(members, count, side, side, width)

    def second(index):
        member = index // count
        tile = index % count
        tiles = grad_lows[member]
        padded = frame_from(tiles, neighbors[tile], tiles[tile], margin)
        back = transposed(padded, kernel)
        return (cotangent[member, tile].astype(jnp.float32) + back).astype(jnp.bfloat16)
    state_grad = lax.map(second, jnp.arange(members * count, dtype=jnp.int32)).reshape(members, count, side, side, width)
    new_state = news.reshape(members, count, side, side, width)
    factor = 1.0 / math.sqrt(members * count * side * side)
    grad_win, grad_wout, grad_kern, grad_bin, grad_conv, grad_gain, grad_shift, grad_bout, grad_gamma = totals
    channels = jnp.stack([grad_conv, grad_gain, grad_shift, grad_bout, grad_gamma]) * factor
    return (new_state, state_grad, grad_win * factor, grad_wout * factor, grad_kern * factor, grad_bin * factor, channels)
```

```python
import functools
import math

import jax
import jax.numpy as jnp
from jax import lax
from jax.experimental import pallas as pl
from jax.experimental.pallas import tpu as pltpu
from jax.sharding import PartitionSpec as P

OFFSETS = (1, 2, 3, -1, -2, -3)
GELU_SCALE = 0.7978845608028654
GELU_CUBIC = 0.044715
EPSILON = 1e-06
LANES = 128
LEAD = 8
MESH = pl.DeviceIdType.MESH
F32 = jnp.float32
BF16 = jnp.bfloat16
VMEM_LIMIT = 56 << 20


def vmem_spec():
    return pl.BlockSpec(memory_space=pltpu.VMEM)


def smem_spec():
    return pl.BlockSpec(memory_space=pltpu.SMEM)


def local_params():
    return pltpu.CompilerParams(vmem_limit_bytes=VMEM_LIMIT)


def payload_kernel(side, margin, want_ref, tile_ref, out_ref, wide):
    wide[...] = tile_ref[...].astype(F32)
    edge = side - margin
    for slot in range(len(OFFSETS)):
        for way in range(8):

            @pl.when(want_ref[slot, way] == 1)
            def _():
                for k in range(margin):
                    if way == 0:
                        line = wide[pl.ds(k * side, side), :]
                    elif way == 1:
                        line = wide[pl.ds((edge + k) * side, side), :]
                    elif way == 2:
                        line = wide[pl.ds(k, side, stride=side), :]
                    elif way == 3:
                        line = wide[pl.ds(edge + k, side, stride=side), :]
                    else:
                        row = k if way in (4, 5) else edge + k
                        start = 0 if way in (4, 6) else side - 8
                        line = jnp.concatenate(
                            [wide[pl.ds(row * side + start, 8), :]] * (side // 8), axis=0
                        )
                    out_ref[slot, k] = line.astype(BF16)


def payload(want, tile, side, margin):
    width = tile.shape[1]
    return pl.pallas_call(
        functools.partial(payload_kernel, side, margin),
        grid=(width // LANES,),
        in_specs=[smem_spec(), pl.BlockSpec((side * side, LANES), lambda c: (0, c))],
        out_specs=pl.BlockSpec((len(OFFSETS), margin, side, LANES), lambda c: (0, 0, 0, c)),
        out_shape=jax.ShapeDtypeStruct((len(OFFSETS), margin, side, width), BF16),
        scratch_shapes=[pltpu.VMEM((side * side, LANES), F32)],
        compiler_params=local_params(),
        name="payload",
    )(want, tile)


def exchange_kernel(count, send_ref, recv_ref, send_sem, recv_sem):
    me = lax.axis_index("tile")
    barrier = pltpu.get_barrier_semaphore()
    peers = [lax.rem(me + offset + count, count) for offset in OFFSETS]
    for peer in peers:
        pl.semaphore_signal(barrier, inc=1, device_id={"tile": peer}, device_id_type=MESH)
    pl.semaphore_wait(barrier, len(OFFSETS))
    copies = []
    for slot, peer in enumerate(peers):
        copy = pltpu.make_async_remote_copy(
            src_ref=send_ref.at[slot],
            dst_ref=recv_ref.at[slot],
            send_sem=send_sem.at[slot],
            recv_sem=recv_sem.at[slot],
            device_id={"tile": peer},
            device_id_type=MESH,
        )
        copy.start()
        copies.append(copy)
    for copy in copies:
        copy.wait()


def exchange(pieces, count, ident):
    return pl.pallas_call(
        functools.partial(exchange_kernel, count),
        in_specs=[vmem_spec()],
        out_specs=vmem_spec(),
        out_shape=jax.ShapeDtypeStruct(pieces.shape, pieces.dtype),
        scratch_shapes=[
            pltpu.SemaphoreType.DMA((len(OFFSETS),)),
            pltpu.SemaphoreType.DMA((len(OFFSETS),)),
        ],
        compiler_params=pltpu.CompilerParams(
            collective_id=ident, has_side_effects=True, vmem_limit_bytes=VMEM_LIMIT
        ),
        name="exchange",
    )(pieces)


def stride_of(side):
    return side + 2 * LEAD


def fill(padded, side, margin, have_ref, recv_ref):
    pitch = stride_of(side)
    for slot in range(len(OFFSETS)):
        for way in range(8):

            @pl.when(have_ref[slot, way] == 1)
            def _():
                for k in range(margin):
                    line = recv_ref[slot, k].astype(F32)
                    if way == 0:
                        padded[pl.ds((margin + side + k) * pitch + LEAD, side), :] = line
                    elif way == 1:
                        padded[pl.ds(k * pitch + LEAD, side), :] = line
                    elif way == 2:
                        padded[pl.ds(margin * pitch + LEAD + side + k, side, stride=pitch), :] = line
                    elif way == 3:
                        padded[pl.ds(margin * pitch + LEAD - margin + k, side, stride=pitch), :] = line
                    else:
                        row = margin + side + k if way in (4, 5) else k
                        start = LEAD + side if way in (4, 6) else LEAD - 8
                        padded[pl.ds(row * pitch + start, 8), :] = line[:8]


def place(padded, side, margin, center, have_ref, recv_ref):
    pitch = stride_of(side)
    rows = side + 2 * margin
    padded[...] = jnp.zeros_like(padded)
    for row in range(side):
        padded[pl.ds((margin + row) * pitch + LEAD, side), :] = center(row)
    del rows
    fill(padded, side, margin, have_ref, recv_ref)


def convolve(padded, kern_ref, side, taps, flipped, emit, group=4):
    pitch = stride_of(side)
    margin = taps // 2

    def step(index, carry):
        base = index * group
        total = [jnp.zeros((side, LANES), F32) for _ in range(group)]
        for col in range(taps):
            for row in range(group + taps - 1):
                start = (base + row) * pitch
                line = padded[pl.ds(start + (LEAD - margin + col), side), :]
                for out in range(group):
                    up = row - out
                    if 0 <= up < taps:
                        at = (taps - 1 - up) * taps + taps - 1 - col if flipped else up * taps + col
                        total[out] = total[out] + kern_ref[pl.ds(at, 1), :] * line
        for out in range(group):
            emit(base + out, total[out])
        return carry

    lax.fori_loop(0, side // group, step, 0)


def forward_kernel(side, taps, have_ref, tile_ref, recv_ref, kern_ref, bias_ref, mixed_ref, padded):
    margin = taps // 2

    def center(row):
        return tile_ref[pl.ds(row * side, side), :].astype(F32)

    place(padded, side, margin, center, have_ref, recv_ref)

    def emit(row, value):
        mixed_ref[pl.ds(pl.multiple_of(row * side, side), side), :] = value + bias_ref[...]

    convolve(padded, kern_ref, side, taps, False, emit)


def forward_conv(have, tile, recv, kern, bias, side, taps):
    width = tile.shape[1]
    margin = taps // 2
    cells = side * side
    spread = (side + 2 * margin) * stride_of(side)
    lane = lambda c: (0, c)
    return pl.pallas_call(
        functools.partial(forward_kernel, side, taps),
        grid=(width // LANES,),
        in_specs=[
            smem_spec(),
            pl.BlockSpec((cells, LANES), lane),
            pl.BlockSpec((len(OFFSETS), margin, side, LANES), lambda c: (0, 0, 0, c)),
            pl.BlockSpec((taps * taps, LANES), lane),
            pl.BlockSpec((1, LANES), lane),
        ],
        out_specs=[pl.BlockSpec((cells, LANES), lane), pl.BlockSpec((spread, LANES), lane)],
        out_shape=[
            jax.ShapeDtypeStruct((cells, width), F32),
            jax.ShapeDtypeStruct((spread, width), F32),
        ],
        compiler_params=local_params(),
        name="forward_conv",
    )(have, tile, recv, kern, bias)


def backward_kernel(
    side, taps, have_ref, grad_ref, recv_ref, kern_ref, cot_ref, state_ref, out_ref, gkern_ref, padded
):
    margin = taps // 2
    pitch = stride_of(side)

    def center(row):
        return grad_ref[pl.ds(row * side, side), :].astype(BF16).astype(F32)

    place(padded, side, margin, center, have_ref, recv_ref)

    def emit(row, value):
        at = pl.ds(pl.multiple_of(row * side, side), side)
        out_ref[at, :] = (cot_ref[at, :].astype(F32) + value).astype(BF16)

    convolve(padded, kern_ref, side, taps, True, emit)

    group = 4
    for col in range(taps):

        def step(index, sums):
            sums = list(sums)
            base = index * group
            grads = [
                grad_ref[pl.ds(pl.multiple_of((base + out) * side, side), side), :]
                for out in range(group)
            ]
            for row in range(group + taps - 1):
                line = state_ref[pl.ds((base + row) * pitch + (LEAD - margin + col), side), :]
                for out in range(group):
                    up = row - out
                    if 0 <= up < taps:
                        product = line * grads[out]
                        for part in range(side // 8):
                            sums[up] = sums[up] + product[part * 8 : part * 8 + 8]
            return tuple(sums)

        zero = jnp.zeros((8, LANES), F32)
        sums = lax.fori_loop(0, side // group, step, (zero,) * taps)
        for up in range(taps):
            gkern_ref[pl.ds(up * taps + col, 1), :] = jnp.sum(sums[up], axis=0, keepdims=True)


def backward_conv(have, grad, recv, kern, cot, padded, side, taps):
    width = grad.shape[1]
    margin = taps // 2
    cells = side * side
    spread = (side + 2 * margin) * stride_of(side)
    lane = lambda c: (0, c)
    return pl.pallas_call(
        functools.partial(backward_kernel, side, taps),
        grid=(width // LANES,),
        in_specs=[
            smem_spec(),
            pl.BlockSpec((cells, LANES), lane),
            pl.BlockSpec((len(OFFSETS), margin, side, LANES), lambda c: (0, 0, 0, c)),
            pl.BlockSpec((taps * taps, LANES), lane),
            pl.BlockSpec((cells, LANES), lane),
            pl.BlockSpec((spread, LANES), lane),
        ],
        out_specs=[
            pl.BlockSpec((cells, LANES), lane),
            pl.BlockSpec((taps * taps, LANES), lane),
        ],
        out_shape=[
            jax.ShapeDtypeStruct((cells, width), BF16),
            jax.ShapeDtypeStruct((taps * taps, width), F32),
        ],
        scratch_shapes=[pltpu.VMEM((spread, LANES), F32)],
        compiler_params=local_params(),
        name="backward_conv",
    )(have, grad, recv, kern, cot, padded)


def contract_rows(left, right):
    return lax.dot_general(left, right, (((0,), (0,)), ((), ())), preferred_element_type=F32)


def contract_cols(left, right):
    return lax.dot_general(left, right, (((1,), (1,)), ((), ())), preferred_element_type=F32)


def mlp_kernel(
    chunk,
    mixed_ref,
    state_ref,
    cot_ref,
    win_ref,
    wout_ref,
    bin_ref,
    rows_ref,
    new_ref,
    gmix_ref,
    gw_ref,
    gbin_ref,
    gch_ref,
    acc_ref,
):
    step = pl.program_id(0)
    last = pl.num_programs(0) - 1
    hidden = win_ref.shape[1]
    gain = rows_ref[0:1, :]
    shift = rows_ref[1:2, :]
    bout = rows_ref[2:3, :]
    scale = rows_ref[3:4, :]

    @pl.when(step == 0)
    def _():
        acc_ref[...] = jnp.zeros_like(acc_ref)
        gbin_ref[...] = jnp.zeros_like(gbin_ref)
        gch_ref[...] = jnp.zeros_like(gch_ref)

    mixed = mixed_ref[...]
    centered = mixed - jnp.mean(mixed, axis=1, keepdims=True)
    variance = jnp.mean(centered * centered, axis=1, keepdims=True)
    inv_std = lax.rsqrt(variance + EPSILON)
    norm_hat = centered * inv_std
    normed = (norm_hat * gain + shift).astype(BF16)
    cot = cot_ref[...].astype(F32)
    grad_branch = scale * cot
    branch_low = grad_branch.astype(BF16)

    branch = jnp.zeros_like(mixed)
    grad_normed = jnp.zeros_like(mixed)
    for at in range(0, hidden, chunk):
        win = win_ref[:, at : at + chunk]
        wout = wout_ref[at : at + chunk, :]
        pre = jnp.dot(normed, win, preferred_element_type=F32) + bin_ref[:, at : at + chunk]
        square = pre * pre
        tanh_value = jnp.tanh(GELU_SCALE * pre * (1.0 + GELU_CUBIC * square))
        half = 0.5 * (1.0 + tanh_value)
        activation = (pre * half).astype(BF16)
        slope = half + (0.5 * GELU_SCALE) * pre * (1.0 - tanh_value * tanh_value) * (
            1.0 + 3.0 * GELU_CUBIC * square
        )
        grad_pre = contract_cols(branch_low, wout) * slope
        grad_low = grad_pre.astype(BF16)
        branch = branch + jnp.dot(activation, wout, preferred_element_type=F32)
        grad_normed = grad_normed + contract_cols(grad_low, win)
        acc_ref[0, at : at + chunk, :] += contract_rows(grad_low, normed)
        acc_ref[1, at : at + chunk, :] += contract_rows(activation, branch_low)
        gbin_ref[:, at : at + chunk] += jnp.sum(grad_pre, axis=0, keepdims=True)

    branch = branch + bout
    new_ref[...] = (state_ref[...].astype(F32) + scale * branch).astype(BF16)
    scaled = grad_normed * gain
    grad_mixed = inv_std * (
        scaled
        - jnp.mean(scaled, axis=1, keepdims=True)
        - norm_hat * jnp.mean(scaled * norm_hat, axis=1, keepdims=True)
    )
    gmix_ref[...] = grad_mixed
    gch_ref[0:1, :] += jnp.sum(grad_mixed, axis=0, keepdims=True)
    gch_ref[1:2, :] += jnp.sum(grad_normed * norm_hat, axis=0, keepdims=True)
    gch_ref[2:3, :] += jnp.sum(grad_normed, axis=0, keepdims=True)
    gch_ref[3:4, :] += jnp.sum(grad_branch, axis=0, keepdims=True)
    gch_ref[4:5, :] += jnp.sum(cot * branch, axis=0, keepdims=True)

    @pl.when(step == last)
    def _():
        gw_ref[...] = acc_ref[...].astype(BF16)


def pointwise(mixed, state, cot, w_in, w_out, bias_in, rows, block=256, chunk=512):
    cells, width = mixed.shape
    hidden = w_in.shape[1]
    cell = lambda r: (r, 0)
    whole = lambda r: (0, 0)
    return pl.pallas_call(
        functools.partial(mlp_kernel, chunk),
        grid=(cells // block,),
        in_specs=[
            pl.BlockSpec((block, width), cell),
            pl.BlockSpec((block, width), cell),
            pl.BlockSpec((block, width), cell),
            pl.BlockSpec((width, hidden), whole),
            pl.BlockSpec((hidden, width), whole),
            pl.BlockSpec((1, hidden), whole),
            pl.BlockSpec(rows.shape, whole),
        ],
        out_specs=[
            pl.BlockSpec((block, width), cell),
            pl.BlockSpec((block, width), cell),
            pl.BlockSpec((2, hidden, width), lambda r: (0, 0, 0)),
            pl.BlockSpec((1, hidden), whole),
            pl.BlockSpec((8, width), whole),
        ],
        out_shape=[
            jax.ShapeDtypeStruct((cells, width), BF16),
            jax.ShapeDtypeStruct((cells, width), F32),
            jax.ShapeDtypeStruct((2, hidden, width), BF16),
            jax.ShapeDtypeStruct((1, hidden), F32),
            jax.ShapeDtypeStruct((8, width), F32),
        ],
        scratch_shapes=[pltpu.VMEM((2, hidden, width), F32)],
        compiler_params=local_params(),
        name="pointwise",
    )(mixed, state, cot, w_in, w_out, bias_in, rows)


def reduce_kernel(
    members,
    tiles,
    big_ref,
    small_ref,
    out_ref,
    sout_ref,
    core_in,
    x_out,
    x_in,
    t_out,
    t_in,
    own,
    sm_in,
    st_out,
    st_in,
    s_own,
    core_sem,
    x_sem,
    t_sem,
    g_sem,
    sm_sem,
    st_sem,
    sg_sem,
):
    member = lax.axis_index("member")
    tile = lax.axis_index("tile")
    core = lax.rem(member, 2)
    cross = member // 2
    spots = members // 2
    mates = [lax.rem(member + k, members) for k in range(1, members)]
    peers = [lax.rem(tile + k, tiles) for k in range(1, tiles)]
    barrier = pltpu.get_barrier_semaphore()
    for mate in mates:
        pl.semaphore_signal(barrier, inc=1, device_id={"member": mate}, device_id_type=MESH)
    for peer in peers:
        pl.semaphore_signal(barrier, inc=1, device_id={"tile": peer}, device_id_type=MESH)
    pl.semaphore_wait(barrier, members + tiles - 2)

    def remote(source, target, sems, slot, **device):
        copy = pltpu.make_async_remote_copy(
            src_ref=source,
            dst_ref=target,
            send_sem=sems.at[0, slot],
            recv_sem=sems.at[1, slot],
            device_id=device,
            device_id_type=MESH,
        )
        copy.start()
        return copy

    pair = [
        remote(big_ref.at[:, :, :, 1 - core], core_in, core_sem, 0, member=cross * 2 + 1 - core)
    ]
    small = [
        remote(small_ref, sm_in.at[k], sm_sem, k, member=mate) for k, mate in enumerate(mates)
    ]
    pair[0].wait()

    def add_pair(t, carry):
        for x in range(spots):
            x_out[x, :, t] = (
                big_ref[:, t, x, core].astype(F32) + core_in[:, t, x].astype(F32)
            ).astype(BF16)
        return carry

    lax.fori_loop(0, tiles, add_pair, 0)
    over = []
    for k in range(1, spots):
        spot = lax.rem(cross + k, spots)
        over.append(remote(x_out.at[spot], x_in.at[k - 1], x_sem, k - 1, member=spot * 2 + core))
    for copy in small:
        copy.wait()
    total = small_ref[...]
    for k in range(members - 1):
        total = total + sm_in[k]
    st_out[...] = total
    small = [
        remote(st_out.at[peer], st_in.at[k], st_sem, k, tile=peer) for k, peer in enumerate(peers)
    ]
    for copy in over:
        copy.wait()

    def add_cross(t, carry):
        value = x_out[cross, :, t].astype(F32)
        for k in range(spots - 1):
            value = value + x_in[k, :, t].astype(F32)
        t_out[t] = value.astype(BF16)
        return carry

    lax.fori_loop(0, tiles, add_cross, 0)
    along = [
        remote(t_out.at[peer], t_in.at[k], t_sem, k, tile=peer) for k, peer in enumerate(peers)
    ]
    for copy in small:
        copy.wait()
    total = st_out[tile]
    for k in range(tiles - 1):
        total = total + st_in[k]
    s_own[...] = total
    small = [
        remote(s_own, sout_ref.at[tile], sg_sem, k, tile=peer) for k, peer in enumerate(peers)
    ]
    sout_ref[tile] = total
    for copy in along:
        copy.wait()
    value = t_out[tile].astype(F32)
    for k in range(tiles - 1):
        value = value + t_in[k].astype(F32)
    own[...] = value.astype(BF16)
    back = [
        remote(own, out_ref.at[member], g_sem, k, member=mate) for k, mate in enumerate(mates)
    ]
    out_ref[member] = own[...]
    for copy in small + back:
        copy.wait()


def reduce_all(big, small, members, tiles):
    _, _, spots, _, rows, width = big.shape
    lines = small.shape[1]
    dma = lambda n: pltpu.SemaphoreType.DMA((2, max(n, 1)))
    return pl.pallas_call(
        functools.partial(reduce_kernel, members, tiles),
        in_specs=[vmem_spec(), vmem_spec()],
        out_specs=[vmem_spec(), vmem_spec()],
        out_shape=[
            jax.ShapeDtypeStruct((members, 2, rows, width), BF16),
            jax.ShapeDtypeStruct((tiles, lines, width), F32),
        ],
        scratch_shapes=[
            pltpu.VMEM((2, tiles, spots, rows, width), BF16),
            pltpu.VMEM((spots, 2, tiles, rows, width), BF16),
            pltpu.VMEM((max(spots - 1, 1), 2, tiles, rows, width), BF16),
            pltpu.VMEM((tiles, 2, rows, width), BF16),
            pltpu.VMEM((tiles - 1, 2, rows, width), BF16),
            pltpu.VMEM((2, rows, width), BF16),
            pltpu.VMEM((members - 1, tiles, lines, width), F32),
            pltpu.VMEM((tiles, lines, width), F32),
            pltpu.VMEM((tiles - 1, lines, width), F32),
            pltpu.VMEM((lines, width), F32),
            dma(1),
            dma(spots - 1),
            dma(tiles - 1),
            dma(members - 1),
            dma(members - 1),
            dma(tiles - 1),
            dma(tiles - 1),
        ],
        compiler_params=pltpu.CompilerParams(
            collective_id=2, has_side_effects=True, vmem_limit_bytes=VMEM_LIMIT
        ),
        name="reduce_all",
    )(big, small)


def body(
    state,
    cotangent,
    neighbors,
    kernel,
    conv_bias,
    norm_gain,
    norm_shift,
    w_in,
    bias_in,
    w_out,
    bias_out,
    layer_scale,
):
    side, width = state.shape[2], state.shape[4]
    cells = side * side
    center = state.reshape(cells, width)
    cot = cotangent.reshape(cells, width)
    hidden = w_in.shape[1]
    taps = kernel.shape[0]
    margin = taps // 2
    count = lax.axis_size("tile")
    members = lax.axis_size("member")
    myself = lax.axis_index("tile")
    steps = jnp.array(OFFSETS, jnp.int32)
    takers = (myself + steps + count) % count
    givers = (myself - steps + count) % count
    want = (neighbors[takers] == myself).astype(jnp.int32)
    have = (neighbors[myself][None, :] == givers[:, None]).astype(jnp.int32)
    flat_kernel = kernel.reshape(taps * taps, width)

    got = exchange(payload(want, center, side, margin), count, 0)
    mixed, padded = forward_conv(have, center, got, flat_kernel, conv_bias[None], side, taps)
    vectors = jnp.stack([norm_gain, norm_shift, bias_out, layer_scale] * 2)
    new_tile, grad_mixed, grad_w, grad_bin, grad_ch = pointwise(
        mixed, center, cot, w_in, w_out, bias_in[None], vectors
    )
    got_grad = exchange(payload(want, grad_mixed, side, margin), count, 1)
    state_grad, grad_kern = backward_conv(
        have, grad_mixed, got_grad, flat_kernel, cot, padded, side, taps
    )

    share = hidden // count
    rows = share // members
    big = grad_w.reshape(2, count, members // 2, 2, rows, width)
    parts = [grad_kern, grad_bin.reshape(hidden // width, width), grad_ch]
    packed = jnp.concatenate(parts, axis=0)
    lines = 8 * (-(-packed.shape[0] // (8 * count)))
    packed = jnp.pad(packed, ((0, lines * count - packed.shape[0]), (0, 0)))
    big, small = reduce_all(big, packed.reshape(count, lines, width), members, count)
    factor = 1.0 / math.sqrt(members * count * cells)
    big = big.astype(F32) * factor
    win_share = big[:, 0].reshape(share, width).T
    wout_share = big[:, 1].reshape(share, width)
    small = small.reshape(count * lines, width) * factor
    first = taps * taps
    second = first + hidden // width
    return (
        new_tile.reshape(state.shape),
        state_grad.reshape(state.shape),
        win_share,
        wout_share,
        small[:first].reshape(taps, taps, width),
        small[first:second].reshape(hidden),
        small[second : second + 5],
    )


def solution(mesh):
    tiled = P("member", "tile", None, None, None)
    in_specs = (tiled, tiled) + (P(),) * 10
    out_specs = (tiled, tiled, P(None, "tile"), P("tile", None), P(), P(), P())
    return jax.shard_map(body, mesh=mesh, in_specs=in_specs, out_specs=out_specs, check_vma=False)
```

```python
import functools
import math

import jax
import jax.numpy as jnp
from jax import lax
from jax.experimental import pallas as pl
from jax.experimental.pallas import tpu as pltpu
from jax.sharding import PartitionSpec as P

OFFSETS = (1, 2, 3, -1, -2, -3)
GELU_SCALE = 0.7978845608028654
GELU_CUBIC = 0.044715
EPSILON = 1e-06
LANES = 128
LEAD = 8
MESH = pl.DeviceIdType.MESH
F32 = jnp.float32
BF16 = jnp.bfloat16
VMEM_LIMIT = 56 << 20


def vmem_spec():
    return pl.BlockSpec(memory_space=pltpu.VMEM)


def smem_spec():
    return pl.BlockSpec(memory_space=pltpu.SMEM)


def local_params():
    return pltpu.CompilerParams(vmem_limit_bytes=VMEM_LIMIT)


def remote_params(ident):
    return pltpu.CompilerParams(
        collective_id=ident, has_side_effects=True, vmem_limit_bytes=VMEM_LIMIT
    )


def pitch_of(side):
    return side + 2 * LEAD


def spread_of(side, margin):
    return (side + 2 * margin) * pitch_of(side)


def place(padded, side, margin, center):
    pitch = pitch_of(side)
    for part in range(padded.shape[0]):

        def clear(row, carry):
            at = pl.ds(pl.multiple_of(row * pitch, 8), pitch)
            padded[part, at, :] = jnp.zeros((pitch, LANES), F32)
            return carry

        lax.fori_loop(0, side + 2 * margin, clear, 0)

        def put(row, carry):
            at = pl.ds(pl.multiple_of((margin + row) * pitch + LEAD, 8), side)
            padded[part, at, :] = center(part, row)
            return carry

        lax.fori_loop(0, side, put, 0)


def around(tile, count):
    takers = [lax.rem(tile + offset + count, count) for offset in OFFSETS]
    givers = [lax.rem(tile - offset + count, count) for offset in OFFSETS]
    return takers, givers


def pack(padded, side, margin, want, send_ref):
    pitch = pitch_of(side)
    edge = side - margin
    for part in range(padded.shape[0]):
        lanes = pl.ds(part * LANES, LANES)
        for k in range(margin):
            low = (margin + k) * pitch + LEAD
            high = (margin + edge + k) * pitch + LEAD
            first = margin * pitch + LEAD
            lines = [
                padded[part, pl.ds(low, side), :],
                padded[part, pl.ds(high, side), :],
                padded[part, pl.ds(first + k, side, stride=pitch), :],
                padded[part, pl.ds(first + edge + k, side, stride=pitch), :],
            ]
            lines = lines + [
                jnp.concatenate([lines[0][:8]] * (side // 8), axis=0),
                jnp.concatenate([lines[0][side - 8 :]] * (side // 8), axis=0),
                jnp.concatenate([lines[1][:8]] * (side // 8), axis=0),
                jnp.concatenate([lines[1][side - 8 :]] * (side // 8), axis=0),
            ]
            for slot in range(len(OFFSETS)):
                line = lines[7]
                for way in range(7):
                    line = jnp.where(want[slot][way], lines[way], line)
                send_ref[slot, k, :, lanes] = line.astype(BF16)


def unpack(padded, side, margin, have, recv_ref):
    pitch = pitch_of(side)
    for part in range(padded.shape[0]):
        lanes = pl.ds(part * LANES, LANES)
        for k in range(margin):
            lines = [recv_ref[slot, k, :, lanes].astype(F32) for slot in range(len(OFFSETS))]
            for way in range(8):
                size = side if way < 4 else 8
                line = jnp.zeros((size, LANES), F32)
                for slot in range(len(OFFSETS)):
                    line = jnp.where(have[slot][way], lines[slot][:size], line)
                if way == 0:
                    at = pl.ds((margin + side + k) * pitch + LEAD, side)
                elif way == 1:
                    at = pl.ds(k * pitch + LEAD, side)
                elif way == 2:
                    at = pl.ds(margin * pitch + LEAD + side + k, side, stride=pitch)
                elif way == 3:
                    at = pl.ds(margin * pitch + LEAD - margin + k, side, stride=pitch)
                else:
                    row = margin + side + k if way in (4, 5) else k
                    at = pl.ds(row * pitch + (LEAD + side if way in (4, 6) else LEAD - 8), 8)
                padded[part, at, :] = line


def convolve(padded, part, kern_ref, side, taps, flipped, emit, group=4):
    pitch = pitch_of(side)
    margin = taps // 2
    lanes = pl.ds(part * LANES, LANES)

    def step(index, carry):
        base = index * group
        total = [jnp.zeros((side, LANES), F32) for _ in range(group)]
        for col in range(taps):
            for row in range(group + taps - 1):
                start = (base + row) * pitch
                line = padded[part, pl.ds(start + (LEAD - margin + col), side), :]
                for out in range(group):
                    up = row - out
                    if 0 <= up < taps:
                        a, b = (taps - 1 - up, taps - 1 - col) if flipped else (up, col)
                        total[out] = total[out] + kern_ref[a, pl.ds(b, 1), lanes] * line
        for out in range(group):
            emit(pl.multiple_of((base + out) * side, side), total[out])
        return carry

    lax.fori_loop(0, side // group, step, 0)


def kernel_grad(padded, part, grad_ref, side, taps, emit, group=4):
    pitch = pitch_of(side)
    margin = taps // 2
    for col in range(taps):

        def step(index, sums):
            sums = list(sums)
            base = index * group
            grads = [
                grad_ref[part, pl.ds(pl.multiple_of((base + out) * side, side), side), :]
                for out in range(group)
            ]
            for row in range(group + taps - 1):
                start = (base + row) * pitch
                line = padded[part, pl.ds(start + (LEAD - margin + col), side), :]
                for out in range(group):
                    up = row - out
                    if 0 <= up < taps:
                        product = line * grads[out]
                        for piece in range(side // 8):
                            sums[up] = sums[up] + product[piece * 8 : piece * 8 + 8]
            return tuple(sums)

        zero = jnp.zeros((8, LANES), F32)
        sums = lax.fori_loop(0, side // group, step, (zero,) * taps)
        for up in range(taps):
            emit(up, col, jnp.sum(sums[up], axis=0, keepdims=True))


def remote(source, target, sems, slot, **device):
    copy = pltpu.make_async_remote_copy(
        src_ref=source,
        dst_ref=target,
        send_sem=sems.at[0, slot],
        recv_sem=sems.at[1, slot],
        device_id=device,
        device_id_type=MESH,
    )
    copy.start()
    return copy


def swap_halo(padded, side, margin, links_ref, send_ref, recv_ref, sems, count, ready):
    tile = lax.axis_index("tile")
    takers, _ = around(tile, count)
    want = [[links_ref[taker, way] == tile for way in range(8)] for taker in takers]
    pack(padded, side, margin, want, send_ref)
    ready()
    return [
        remote(send_ref.at[slot], recv_ref.at[slot], sems, slot, tile=taker)
        for slot, taker in enumerate(takers)
    ]


def take_halo(padded, side, margin, links_ref, recv_ref, count):
    tile = lax.axis_index("tile")
    _, givers = around(tile, count)
    have = [[links_ref[tile, way] == giver for way in range(8)] for giver in givers]
    unpack(padded, side, margin, have, recv_ref)


def forward_kernel(
    side, taps, count, links_ref, tile_ref, kern_ref, bias_ref, mixed_ref, padded, send, recv, sems
):
    margin = taps // 2
    barrier = pltpu.get_barrier_semaphore()
    takers, _ = around(lax.axis_index("tile"), count)
    for taker in takers:
        pl.semaphore_signal(barrier, inc=1, device_id={"tile": taker}, device_id_type=MESH)

    def center(part, row):
        at = pl.ds(pl.multiple_of(row * side, side), side)
        return tile_ref[at, pl.ds(part * LANES, LANES)].astype(F32)

    place(padded, side, margin, center)
    copies = swap_halo(
        padded, side, margin, links_ref, send, recv, sems, count,
        lambda: pl.semaphore_wait(barrier, len(OFFSETS)),
    )
    for copy in copies:
        copy.wait()
    take_halo(padded, side, margin, links_ref, recv, count)
    for part in range(padded.shape[0]):
        lanes = pl.ds(part * LANES, LANES)
        bias = bias_ref[lanes].reshape(1, LANES)

        def emit(start, value):
            mixed_ref[pl.ds(start, side), lanes] = value + bias

        convolve(padded, part, kern_ref, side, taps, False, emit)


def halo_scratch(side, margin, width):
    pieces = (len(OFFSETS), margin, side, width)
    return [
        pltpu.VMEM(pieces, BF16),
        pltpu.VMEM(pieces, BF16),
        pltpu.SemaphoreType.DMA((2, len(OFFSETS))),
    ]


def forward_conv(links, tile, kern, bias, side, taps, count):
    cells, width = tile.shape
    margin = taps // 2
    return pl.pallas_call(
        functools.partial(forward_kernel, side, taps, count),
        in_specs=[smem_spec()] + [vmem_spec()] * 3,
        out_specs=[vmem_spec()] * 2,
        out_shape=[
            jax.ShapeDtypeStruct((cells, width), F32),
            jax.ShapeDtypeStruct((width // LANES, spread_of(side, margin), LANES), F32),
        ],
        scratch_shapes=halo_scratch(side, margin, width),
        compiler_params=remote_params(0),
        name="forward_conv",
    )(links, tile, kern, bias)


def contract_rows(left, right):
    return lax.dot_general(left, right, (((0,), (0,)), ((), ())), preferred_element_type=F32)


def contract_cols(left, right):
    return lax.dot_general(left, right, (((1,), (1,)), ((), ())), preferred_element_type=F32)


def mlp_kernel(
    chunk,
    mixed_ref,
    state_ref,
    cot_ref,
    win_ref,
    wout_ref,
    bin_ref,
    gain_ref,
    shift_ref,
    bout_ref,
    scale_ref,
    new_ref,
    gmix_ref,
    gw_ref,
    gbin_ref,
    gch_ref,
    acc_ref,
):
    step = pl.program_id(0)
    last = pl.num_programs(0) - 1
    hidden = win_ref.shape[1]
    gain, shift, bout, scale = (
        ref[...].reshape(1, -1) for ref in (gain_ref, shift_ref, bout_ref, scale_ref)
    )

    @pl.when(step == 0)
    def _():
        acc_ref[...] = jnp.zeros_like(acc_ref)
        gbin_ref[...] = jnp.zeros_like(gbin_ref)
        gch_ref[...] = jnp.zeros_like(gch_ref)

    mixed = mixed_ref[...]
    centered = mixed - jnp.mean(mixed, axis=1, keepdims=True)
    variance = jnp.mean(centered * centered, axis=1, keepdims=True)
    inv_std = lax.rsqrt(variance + EPSILON)
    norm_hat = centered * inv_std
    normed = (norm_hat * gain + shift).astype(BF16)
    cot = cot_ref[...].astype(F32)
    grad_branch = scale * cot
    branch_low = grad_branch.astype(BF16)

    branch = jnp.zeros_like(mixed)
    grad_normed = jnp.zeros_like(mixed)
    for at in range(0, hidden, chunk):
        win = win_ref[:, at : at + chunk]
        wout = wout_ref[at : at + chunk, :]
        pre = jnp.dot(normed, win, preferred_element_type=F32) + bin_ref[pl.ds(at, chunk)].reshape(1, chunk)
        square = pre * pre
        tanh_value = jnp.tanh(GELU_SCALE * pre * (1.0 + GELU_CUBIC * square))
        half = 0.5 * (1.0 + tanh_value)
        activation = (pre * half).astype(BF16)
        slope = half + (0.5 * GELU_SCALE) * pre * (1.0 - tanh_value * tanh_value) * (
            1.0 + 3.0 * GELU_CUBIC * square
        )
        grad_pre = contract_cols(branch_low, wout) * slope
        grad_low = grad_pre.astype(BF16)
        branch = branch + jnp.dot(activation, wout, preferred_element_type=F32)
        grad_normed = grad_normed + contract_cols(grad_low, win)
        acc_ref[0, at : at + chunk, :] += contract_rows(grad_low, normed)
        acc_ref[1, at : at + chunk, :] += contract_rows(activation, branch_low)
        gbin_ref[:, at : at + chunk] += jnp.sum(grad_pre, axis=0, keepdims=True)

    branch = branch + bout
    new_ref[...] = (state_ref[...].astype(F32) + scale * branch).astype(BF16)
    scaled = grad_normed * gain
    grad_mixed = inv_std * (
        scaled
        - jnp.mean(scaled, axis=1, keepdims=True)
        - norm_hat * jnp.mean(scaled * norm_hat, axis=1, keepdims=True)
    )
    for part in range(gmix_ref.shape[0]):
        gmix_ref[part] = grad_mixed[:, part * LANES : (part + 1) * LANES]
    gch_ref[0:1, :] += jnp.sum(grad_mixed, axis=0, keepdims=True)
    gch_ref[1:2, :] += jnp.sum(grad_normed * norm_hat, axis=0, keepdims=True)
    gch_ref[2:3, :] += jnp.sum(grad_normed, axis=0, keepdims=True)
    gch_ref[3:4, :] += jnp.sum(grad_branch, axis=0, keepdims=True)
    gch_ref[4:5, :] += jnp.sum(cot * branch, axis=0, keepdims=True)

    @pl.when(step == last)
    def _():
        gw_ref[...] = acc_ref[...].astype(BF16)


def pointwise(mixed, state, cot, w_in, w_out, bias_in, vectors, block=256, chunk=512):
    cells, width = mixed.shape
    hidden = w_in.shape[1]
    cell = lambda r: (r, 0)
    whole = lambda r: (0, 0)
    return pl.pallas_call(
        functools.partial(mlp_kernel, chunk),
        grid=(cells // block,),
        in_specs=[
            pl.BlockSpec((block, width), cell),
            pl.BlockSpec((block, width), cell),
            pl.BlockSpec((block, width), cell),
            pl.BlockSpec((width, hidden), whole),
            pl.BlockSpec((hidden, width), whole),
            pl.BlockSpec((hidden,), lambda r: (0,)),
        ]
        + [pl.BlockSpec((width,), lambda r: (0,))] * 4,
        out_specs=[
            pl.BlockSpec((block, width), cell),
            pl.BlockSpec((width // LANES, block, LANES), lambda r: (0, r, 0)),
            pl.BlockSpec((2, hidden, width), lambda r: (0, 0, 0)),
            pl.BlockSpec((1, hidden), whole),
            pl.BlockSpec((8, width), whole),
        ],
        out_shape=[
            jax.ShapeDtypeStruct((cells, width), BF16),
            jax.ShapeDtypeStruct((width // LANES, cells, LANES), F32),
            jax.ShapeDtypeStruct((2, hidden, width), BF16),
            jax.ShapeDtypeStruct((1, hidden), F32),
            jax.ShapeDtypeStruct((8, width), F32),
        ],
        scratch_shapes=[pltpu.VMEM((2, hidden, width), F32)],
        compiler_params=local_params(),
        name="pointwise",
    )(mixed, state, cot, w_in, w_out, bias_in, *vectors)


def backward_kernel(
    side,
    taps,
    members,
    tiles,
    links_ref,
    grad_ref,
    kern_ref,
    cot_ref,
    state_ref,
    gbin_ref,
    gch_ref,
    big_ref,
    sgrad_ref,
    out_ref,
    sout_ref,
    padded,
    send,
    recv,
    sems,
    core_in,
    x_out,
    x_in,
    t_out,
    t_in,
    own,
    s_pack,
    sm_in,
    st_out,
    st_in,
    s_own,
    core_sem,
    x_sem,
    t_sem,
    g_sem,
    sm_sem,
    st_sem,
    sg_sem,
):
    margin = taps // 2
    parts = padded.shape[0]
    member = lax.axis_index("member")
    tile = lax.axis_index("tile")
    core = lax.rem(member, 2)
    cross = member // 2
    spots = members // 2
    mates = [lax.rem(member + k, members) for k in range(1, members)]
    peers = [lax.rem(tile + k, tiles) for k in range(1, tiles)]
    barrier = pltpu.get_barrier_semaphore()
    for mate in mates:
        pl.semaphore_signal(barrier, inc=1, device_id={"member": mate}, device_id_type=MESH)
    for peer in peers:
        pl.semaphore_signal(barrier, inc=1, device_id={"tile": peer}, device_id_type=MESH)

    def center(part, row):
        at = pl.ds(pl.multiple_of(row * side, side), side)
        return grad_ref[part, at, :].astype(BF16).astype(F32)

    place(padded, side, margin, center)
    halo = swap_halo(
        padded, side, margin, links_ref, send, recv, sems, tiles,
        lambda: pl.semaphore_wait(barrier, members + tiles - 2),
    )
    pair = [
        remote(
            big_ref.at[kind, :, :, 1 - core], core_in.at[kind], core_sem, kind,
            member=cross * 2 + 1 - core,
        )
        for kind in range(2)
    ]

    lines = s_pack.shape[1]
    s_pack[...] = jnp.zeros_like(s_pack)
    width = s_pack.shape[2]
    first = taps * taps
    extra = gbin_ref.shape[1] // width
    for row in range(extra):
        at = first + row
        s_pack[at // lines, pl.ds(at % lines, 1), :] = gbin_ref[:, pl.ds(row * width, width)]
    for row in range(5):
        at = first + extra + row
        s_pack[at // lines, pl.ds(at % lines, 1), :] = gch_ref[pl.ds(row, 1), :]

    def own_kernel(part):
        def emit(up, col, value):
            at = up * taps + col
            s_pack[at // lines, pl.ds(at % lines, 1), pl.ds(part * LANES, LANES)] = value

        kernel_grad(state_ref, part, grad_ref, side, taps, emit)

    def conv(part):
        lanes = pl.ds(part * LANES, LANES)

        def emit(start, value):
            at = pl.ds(start, side)
            sgrad_ref[at, lanes] = (cot_ref[at, lanes].astype(F32) + value).astype(BF16)

        convolve(padded, part, kern_ref, side, taps, True, emit)

    def cross_over(kind):
        pair[kind].wait()

        def add(t, carry):
            for x in range(spots):
                mine = big_ref[kind, t, x, core].astype(F32)
                x_out[kind, x, t] = (mine + core_in[kind, t, x].astype(F32)).astype(BF16)
            return carry

        lax.fori_loop(0, tiles, add, 0)
        copies = []
        for k in range(1, spots):
            spot = lax.rem(cross + k, spots)
            copies.append(
                remote(
                    x_out.at[kind, spot], x_in.at[kind, k - 1], x_sem, kind * (spots - 1) + k - 1,
                    member=spot * 2 + core,
                )
            )
        return copies

    def go_along(kind, copies):
        for copy in copies:
            copy.wait()

        def add(t, carry):
            value = x_out[kind, cross, t].astype(F32)
            for k in range(spots - 1):
                value = value + x_in[kind, k, t].astype(F32)
            t_out[kind, t] = value.astype(BF16)
            return carry

        lax.fori_loop(0, tiles, add, 0)
        return [
            remote(
                t_out.at[kind, peer], t_in.at[kind, k], t_sem, kind * (tiles - 1) + k, tile=peer
            )
            for k, peer in enumerate(peers)
        ]

    def send_back(kind, copies):
        for copy in copies:
            copy.wait()
        value = t_out[kind, tile].astype(F32)
        for k in range(tiles - 1):
            value = value + t_in[kind, k].astype(F32)
        own[kind] = value.astype(BF16)
        out_ref[kind, member] = value.astype(BF16)
        return [
            remote(
                own.at[kind], out_ref.at[kind, member], g_sem, kind * (members - 1) + k, member=mate
            )
            for k, mate in enumerate(mates)
        ]

    own_kernel(0)
    over = [cross_over(0)]
    own_kernel(1)
    over.append(cross_over(1))
    for part in range(2, parts):
        own_kernel(part)
    small = [remote(s_pack, sm_in.at[k], sm_sem, k, member=mate) for k, mate in enumerate(mates)]
    for copy in halo:
        copy.wait()
    take_halo(padded, side, margin, links_ref, recv, tiles)
    conv(0)
    along = [go_along(0, over[0])]
    conv(1)
    along.append(go_along(1, over[1]))
    for copy in small:
        copy.wait()
    total = s_pack[...]
    for k in range(members - 1):
        total = total + sm_in[k]
    st_out[...] = total
    small = [
        remote(st_out.at[peer], st_in.at[k], st_sem, k, tile=peer) for k, peer in enumerate(peers)
    ]
    for part in range(2, parts):
        conv(part)
    back = send_back(0, along[0])
    for copy in small:
        copy.wait()
    total = st_out[tile]
    for k in range(tiles - 1):
        total = total + st_in[k]
    s_own[...] = total
    sout_ref[tile] = total
    small = [
        remote(s_own, sout_ref.at[tile], sg_sem, k, tile=peer) for k, peer in enumerate(peers)
    ]
    back = back + send_back(1, along[1])
    for copy in small + back:
        copy.wait()


def backward_all(links, grad, kern, cot, padded, grad_bin, grad_ch, big, side, members, tiles):
    _, _, spots, _, rows, width = big.shape
    taps = kern.shape[0]
    margin = taps // 2
    used = taps * taps + grad_bin.shape[1] // width + 5
    lines = 8 * (-(-used // (8 * tiles)))
    dma = lambda n: pltpu.SemaphoreType.DMA((2, max(n, 1)))
    return pl.pallas_call(
        functools.partial(backward_kernel, side, taps, members, tiles),
        in_specs=[smem_spec()] + [vmem_spec()] * 7,
        out_specs=[vmem_spec()] * 3,
        out_shape=[
            jax.ShapeDtypeStruct(cot.shape, BF16),
            jax.ShapeDtypeStruct((2, members, rows, width), BF16),
            jax.ShapeDtypeStruct((tiles, lines, width), F32),
        ],
        scratch_shapes=[pltpu.VMEM(padded.shape, F32)]
        + halo_scratch(side, margin, width)
        + [
            pltpu.VMEM((2, tiles, spots, rows, width), BF16),
            pltpu.VMEM((2, spots, tiles, rows, width), BF16),
            pltpu.VMEM((2, max(spots - 1, 1), tiles, rows, width), BF16),
            pltpu.VMEM((2, tiles, rows, width), BF16),
            pltpu.VMEM((2, tiles - 1, rows, width), BF16),
            pltpu.VMEM((2, rows, width), BF16),
            pltpu.VMEM((tiles, lines, width), F32),
            pltpu.VMEM((members - 1, tiles, lines, width), F32),
            pltpu.VMEM((tiles, lines, width), F32),
            pltpu.VMEM((tiles - 1, lines, width), F32),
            pltpu.VMEM((lines, width), F32),
            dma(2),
            dma(2 * (spots - 1)),
            dma(2 * (tiles - 1)),
            dma(2 * (members - 1)),
            dma(members - 1),
            dma(tiles - 1),
            dma(tiles - 1),
        ],
        compiler_params=remote_params(1),
        name="backward_all",
    )(links, grad, kern, cot, padded, grad_bin, grad_ch, big)


def body(
    state,
    cotangent,
    neighbors,
    kernel,
    conv_bias,
    norm_gain,
    norm_shift,
    w_in,
    bias_in,
    w_out,
    bias_out,
    layer_scale,
):
    side, width = state.shape[2], state.shape[4]
    cells = side * side
    center = state.reshape(cells, width)
    cot = cotangent.reshape(cells, width)
    hidden = w_in.shape[1]
    taps = kernel.shape[0]
    tiles = lax.axis_size("tile")
    members = lax.axis_size("member")
    mixed, padded = forward_conv(neighbors, center, kernel, conv_bias, side, taps, tiles)
    vectors = (norm_gain, norm_shift, bias_out, layer_scale)
    new_tile, grad_mixed, grad_w, grad_bin, grad_ch = pointwise(
        mixed, center, cot, w_in, w_out, bias_in, vectors
    )
    share = hidden // tiles
    rows = share // members
    big = grad_w.reshape(2, tiles, members // 2, 2, rows, width)
    state_grad, big, small = backward_all(
        neighbors, grad_mixed, kernel, cot, padded, grad_bin, grad_ch, big, side, members, tiles
    )
    factor = 1.0 / math.sqrt(members * tiles * cells)
    big = big.astype(F32) * factor
    win_share = big[0].reshape(share, width).T
    wout_share = big[1].reshape(share, width)
    small = small.reshape(-1, width) * factor
    first = taps * taps
    second = first + hidden // width
    return (
        new_tile.reshape(state.shape),
        state_grad.reshape(state.shape),
        win_share,
        wout_share,
        small[:first].reshape(taps, taps, width),
        small[first:second].reshape(hidden),
        small[second : second + 5],
    )


def solution(mesh):
    tiled = P("member", "tile", None, None, None)
    in_specs = (tiled, tiled) + (P(),) * 10
    out_specs = (tiled, tiled, P(None, "tile"), P("tile", None), P(), P(), P())
    return jax.shard_map(body, mesh=mesh, in_specs=in_specs, out_specs=out_specs, check_vma=False)
```

```python
import functools
import math

import jax
import jax.numpy as jnp
from jax import lax
from jax.experimental import pallas as pl
from jax.experimental.pallas import tpu as pltpu
from jax.sharding import PartitionSpec as P

OFFSETS = (1, 2, 3, -1, -2, -3)
GELU_SCALE = 0.7978845608028654
GELU_CUBIC = 0.044715
EPSILON = 1e-06
LANES = 128
LEAD = 8
MESH = pl.DeviceIdType.MESH
F32 = jnp.float32
BF16 = jnp.bfloat16
VMEM_LIMIT = 56 << 20


def vmem_spec():
    return pl.BlockSpec(memory_space=pltpu.VMEM)


def smem_spec():
    return pl.BlockSpec(memory_space=pltpu.SMEM)


def local_params():
    return pltpu.CompilerParams(vmem_limit_bytes=VMEM_LIMIT)


def remote_params(ident):
    return pltpu.CompilerParams(
        collective_id=ident, has_side_effects=True, vmem_limit_bytes=VMEM_LIMIT
    )


def pitch_of(side):
    return side + 2 * LEAD


def spread_of(side, margin):
    return (side + 2 * margin) * pitch_of(side)


def place(padded, side, margin, center):
    pitch = pitch_of(side)
    for part in range(padded.shape[0]):

        def clear(row, carry):
            at = pl.ds(pl.multiple_of(row * pitch, 8), pitch)
            padded[part, at, :] = jnp.zeros((pitch, LANES), F32)
            return carry

        lax.fori_loop(0, side + 2 * margin, clear, 0)

        def put(row, carry):
            at = pl.ds(pl.multiple_of((margin + row) * pitch + LEAD, 8), side)
            padded[part, at, :] = center(part, row)
            return carry

        lax.fori_loop(0, side, put, 0)


def around(tile, count):
    takers = [lax.rem(tile + offset + count, count) for offset in OFFSETS]
    givers = [lax.rem(tile - offset + count, count) for offset in OFFSETS]
    return takers, givers


def pack(padded, side, margin, want, send_ref):
    pitch = pitch_of(side)
    edge = side - margin
    for part in range(padded.shape[0]):
        lanes = pl.ds(part * LANES, LANES)
        for k in range(margin):
            low = (margin + k) * pitch + LEAD
            high = (margin + edge + k) * pitch + LEAD
            first = margin * pitch + LEAD
            lines = [
                padded[part, pl.ds(low, side), :],
                padded[part, pl.ds(high, side), :],
                padded[part, pl.ds(first + k, side, stride=pitch), :],
                padded[part, pl.ds(first + edge + k, side, stride=pitch), :],
            ]
            lines = lines + [
                jnp.concatenate([lines[0][:8]] * (side // 8), axis=0),
                jnp.concatenate([lines[0][side - 8 :]] * (side // 8), axis=0),
                jnp.concatenate([lines[1][:8]] * (side // 8), axis=0),
                jnp.concatenate([lines[1][side - 8 :]] * (side // 8), axis=0),
            ]
            for slot in range(len(OFFSETS)):
                line = lines[7]
                for way in range(7):
                    line = jnp.where(want[slot][way], lines[way], line)
                send_ref[slot, k, :, lanes] = line.astype(BF16)


def unpack(padded, side, margin, have, recv_ref):
    pitch = pitch_of(side)
    for part in range(padded.shape[0]):
        lanes = pl.ds(part * LANES, LANES)
        for k in range(margin):
            lines = [recv_ref[slot, k, :, lanes].astype(F32) for slot in range(len(OFFSETS))]
            for way in range(8):
                size = side if way < 4 else 8
                line = jnp.zeros((size, LANES), F32)
                for slot in range(len(OFFSETS)):
                    line = jnp.where(have[slot][way], lines[slot][:size], line)
                if way == 0:
                    at = pl.ds((margin + side + k) * pitch + LEAD, side)
                elif way == 1:
                    at = pl.ds(k * pitch + LEAD, side)
                elif way == 2:
                    at = pl.ds(margin * pitch + LEAD + side + k, side, stride=pitch)
                elif way == 3:
                    at = pl.ds(margin * pitch + LEAD - margin + k, side, stride=pitch)
                else:
                    row = margin + side + k if way in (4, 5) else k
                    at = pl.ds(row * pitch + (LEAD + side if way in (4, 6) else LEAD - 8), 8)
                padded[part, at, :] = line


def convolve(padded, part, kern_ref, side, taps, flipped, emit, group=4, first=0, gap=1, steps=None):
    pitch = pitch_of(side)
    margin = taps // 2
    lanes = pl.ds(part * LANES, LANES)

    def step(index, carry):
        base = (first + index * gap) * group
        total = [jnp.zeros((side, LANES), F32) for _ in range(group)]
        for col in range(taps):
            for row in range(group + taps - 1):
                start = (base + row) * pitch
                line = padded[part, pl.ds(start + (LEAD - margin + col), side), :]
                for out in range(group):
                    up = row - out
                    if 0 <= up < taps:
                        a, b = (taps - 1 - up, taps - 1 - col) if flipped else (up, col)
                        total[out] = total[out] + kern_ref[a, pl.ds(b, 1), lanes] * line
        for out in range(group):
            emit(pl.multiple_of((base + out) * side, side), total[out])
        return carry

    lax.fori_loop(0, side // group if steps is None else steps, step, 0)


def edge_columns(sides, part, kern_ref, side, taps, add, group=4):
    margin = taps // 2
    lanes = pl.ds(part * LANES, LANES)

    def step(index, carry):
        base = (1 + index) * group
        for east in range(2):
            total = [jnp.zeros((8, LANES), F32) for _ in range(group)]
            for near in range(margin):
                col = margin + 1 + near if east else near
                shift = 1 + near if east else 8 - margin + near
                for row in range(group + taps - 1):
                    line = sides[east, part, pl.ds((base + row) * 16 + shift, 8), :]
                    for out in range(group):
                        up = row - out
                        if 0 <= up < taps:
                            total[out] = total[out] + kern_ref[up, pl.ds(col, 1), lanes] * line
            for out in range(group):
                start = (base + out) * side + (side - 8 if east else 0)
                add(pl.multiple_of(start, 8), total[out])
        return carry

    lax.fori_loop(0, side // group - 2, step, 0)


def kernel_grad(padded, part, grad_ref, side, taps, emit, group=4):
    pitch = pitch_of(side)
    margin = taps // 2
    for col in range(taps):

        def step(index, sums):
            sums = list(sums)
            base = index * group
            grads = [
                grad_ref[part, pl.ds(pl.multiple_of((base + out) * side, side), side), :]
                for out in range(group)
            ]
            for row in range(group + taps - 1):
                start = (base + row) * pitch
                line = padded[part, pl.ds(start + (LEAD - margin + col), side), :]
                for out in range(group):
                    up = row - out
                    if 0 <= up < taps:
                        product = line * grads[out]
                        for piece in range(side // 8):
                            sums[up] = sums[up] + product[piece * 8 : piece * 8 + 8]
            return tuple(sums)

        zero = jnp.zeros((8, LANES), F32)
        sums = lax.fori_loop(0, side // group, step, (zero,) * taps)
        for up in range(taps):
            emit(up, col, jnp.sum(sums[up], axis=0, keepdims=True))


def remote(source, target, sems, slot, **device):
    copy = pltpu.make_async_remote_copy(
        src_ref=source,
        dst_ref=target,
        send_sem=sems.at[0, slot],
        recv_sem=sems.at[1, slot],
        device_id=device,
        device_id_type=MESH,
    )
    copy.start()
    return copy


def swap_halo(padded, side, margin, links_ref, send_ref, recv_ref, sems, count, ready):
    tile = lax.axis_index("tile")
    takers, _ = around(tile, count)
    want = [[links_ref[taker, way] == tile for way in range(8)] for taker in takers]
    pack(padded, side, margin, want, send_ref)
    ready()
    return [
        remote(send_ref.at[slot], recv_ref.at[slot], sems, slot, tile=taker)
        for slot, taker in enumerate(takers)
    ]


def take_halo(padded, side, margin, links_ref, recv_ref, count):
    tile = lax.axis_index("tile")
    _, givers = around(tile, count)
    have = [[links_ref[tile, way] == giver for way in range(8)] for giver in givers]
    unpack(padded, side, margin, have, recv_ref)


def forward_kernel(
    side, taps, count, links_ref, tile_ref, kern_ref, bias_ref, mixed_ref, padded, send, recv, sems, sides
):
    margin = taps // 2
    barrier = pltpu.get_barrier_semaphore()
    takers, _ = around(lax.axis_index("tile"), count)
    for taker in takers:
        pl.semaphore_signal(barrier, inc=1, device_id={"tile": taker}, device_id_type=MESH)

    def center(part, row):
        at = pl.ds(pl.multiple_of(row * side, side), side)
        return tile_ref[at, pl.ds(part * LANES, LANES)].astype(F32)

    place(padded, side, margin, center)
    copies = swap_halo(
        padded, side, margin, links_ref, send, recv, sems, count,
        lambda: pl.semaphore_wait(barrier, len(OFFSETS)),
    )
    parts = padded.shape[0]
    groups = side // 4
    pitch = pitch_of(side)

    def make_emit(part):
        lanes = pl.ds(part * LANES, LANES)
        bias = bias_ref[lanes].reshape(1, LANES)

        def emit(start, value):
            mixed_ref[pl.ds(start, side), lanes] = value + bias

        return emit

    for part in range(parts):
        convolve(
            padded, part, kern_ref, side, taps, False, make_emit(part), first=1, steps=groups - 2
        )
    for copy in copies:
        copy.wait()
    take_halo(padded, side, margin, links_ref, recv, count)
    for part in range(parts):
        lanes = pl.ds(part * LANES, LANES)

        def frame(row, carry):
            at = pl.ds(pl.multiple_of(row * 16, 8), 8)
            after = pl.ds(pl.multiple_of(row * 16 + 8, 8), 8)
            start = row * pitch + LEAD
            blank = jnp.zeros((8, LANES), F32)
            sides[0, part, at, :] = padded[part, pl.ds(pl.multiple_of(start - 8, 8), 8), :]
            sides[0, part, after, :] = blank
            sides[1, part, at, :] = blank
            sides[1, part, after, :] = padded[part, pl.ds(pl.multiple_of(start + side, 8), 8), :]
            return carry

        lax.fori_loop(0, side + 2 * margin, frame, 0)

        def add(start, value):
            mixed_ref[pl.ds(start, 8), lanes] += value

        convolve(
            padded, part, kern_ref, side, taps, False, make_emit(part), gap=groups - 1, steps=2
        )
        edge_columns(sides, part, kern_ref, side, taps, add)


def halo_scratch(side, margin, width):
    pieces = (len(OFFSETS), margin, side, width)
    return [
        pltpu.VMEM(pieces, BF16),
        pltpu.VMEM(pieces, BF16),
        pltpu.SemaphoreType.DMA((2, len(OFFSETS))),
    ]


def forward_conv(links, tile, kern, bias, side, taps, count):
    cells, width = tile.shape
    margin = taps // 2
    return pl.pallas_call(
        functools.partial(forward_kernel, side, taps, count),
        in_specs=[smem_spec()] + [vmem_spec()] * 3,
        out_specs=[vmem_spec()] * 2,
        out_shape=[
            jax.ShapeDtypeStruct((cells, width), F32),
            jax.ShapeDtypeStruct((width // LANES, spread_of(side, margin), LANES), F32),
        ],
        scratch_shapes=halo_scratch(side, margin, width)
        + [pltpu.VMEM((2, width // LANES, (side + 2 * margin) * 16, LANES), F32)],
        compiler_params=remote_params(0),
        name="forward_conv",
    )(links, tile, kern, bias)


def contract_rows(left, right):
    return lax.dot_general(left, right, (((0,), (0,)), ((), ())), preferred_element_type=F32)


def contract_cols(left, right):
    return lax.dot_general(left, right, (((1,), (1,)), ((), ())), preferred_element_type=F32)


def mlp_kernel(
    chunk,
    mixed_ref,
    state_ref,
    cot_ref,
    win_ref,
    wout_ref,
    bin_ref,
    gain_ref,
    shift_ref,
    bout_ref,
    scale_ref,
    new_ref,
    gmix_ref,
    gw_ref,
    gbin_ref,
    gch_ref,
    acc_ref,
):
    step = pl.program_id(0)
    last = pl.num_programs(0) - 1
    hidden = win_ref.shape[1]
    gain, shift, bout, scale = (
        ref[...].reshape(1, -1) for ref in (gain_ref, shift_ref, bout_ref, scale_ref)
    )

    @pl.when(step == 0)
    def _():
        acc_ref[...] = jnp.zeros_like(acc_ref)
        gbin_ref[...] = jnp.zeros_like(gbin_ref)
        gch_ref[...] = jnp.zeros_like(gch_ref)

    mixed = mixed_ref[...]
    centered = mixed - jnp.mean(mixed, axis=1, keepdims=True)
    variance = jnp.mean(centered * centered, axis=1, keepdims=True)
    inv_std = lax.rsqrt(variance + EPSILON)
    norm_hat = centered * inv_std
    normed = (norm_hat * gain + shift).astype(BF16)
    cot = cot_ref[...].astype(F32)
    grad_branch = scale * cot
    branch_low = grad_branch.astype(BF16)

    branch = jnp.zeros_like(mixed)
    grad_normed = jnp.zeros_like(mixed)
    for at in range(0, hidden, chunk):
        win = win_ref[:, at : at + chunk]
        wout = wout_ref[at : at + chunk, :]
        pre = jnp.dot(normed, win, preferred_element_type=F32) + bin_ref[pl.ds(at, chunk)].reshape(1, chunk)
        square = pre * pre
        tanh_value = jnp.tanh(GELU_SCALE * pre * (1.0 + GELU_CUBIC * square))
        half = 0.5 * (1.0 + tanh_value)
        activation = (pre * half).astype(BF16)
        slope = half + (0.5 * GELU_SCALE) * pre * (1.0 - tanh_value * tanh_value) * (
            1.0 + 3.0 * GELU_CUBIC * square
        )
        grad_pre = contract_cols(branch_low, wout) * slope
        grad_low = grad_pre.astype(BF16)
        branch = branch + jnp.dot(activation, wout, preferred_element_type=F32)
        grad_normed = grad_normed + contract_cols(grad_low, win)
        acc_ref[0, at : at + chunk, :] += contract_rows(grad_low, normed)
        acc_ref[1, at : at + chunk, :] += contract_rows(activation, branch_low)
        gbin_ref[:, at : at + chunk] += jnp.sum(grad_pre, axis=0, keepdims=True)

    branch = branch + bout
    new_ref[...] = (state_ref[...].astype(F32) + scale * branch).astype(BF16)
    scaled = grad_normed * gain
    grad_mixed = inv_std * (
        scaled
        - jnp.mean(scaled, axis=1, keepdims=True)
        - norm_hat * jnp.mean(scaled * norm_hat, axis=1, keepdims=True)
    )
    for part in range(gmix_ref.shape[0]):
        gmix_ref[part] = grad_mixed[:, part * LANES : (part + 1) * LANES]
    gch_ref[0:1, :] += jnp.sum(grad_mixed, axis=0, keepdims=True)
    gch_ref[1:2, :] += jnp.sum(grad_normed * norm_hat, axis=0, keepdims=True)
    gch_ref[2:3, :] += jnp.sum(grad_normed, axis=0, keepdims=True)
    gch_ref[3:4, :] += jnp.sum(grad_branch, axis=0, keepdims=True)
    gch_ref[4:5, :] += jnp.sum(cot * branch, axis=0, keepdims=True)

    @pl.when(step == last)
    def _():
        gw_ref[...] = acc_ref[...].astype(BF16)


def pointwise(mixed, state, cot, w_in, w_out, bias_in, vectors, block=256, chunk=512):
    cells, width = mixed.shape
    hidden = w_in.shape[1]
    cell = lambda r: (r, 0)
    whole = lambda r: (0, 0)
    return pl.pallas_call(
        functools.partial(mlp_kernel, chunk),
        grid=(cells // block,),
        in_specs=[
            pl.BlockSpec((block, width), cell),
            pl.BlockSpec((block, width), cell),
            pl.BlockSpec((block, width), cell),
            pl.BlockSpec((width, hidden), whole),
            pl.BlockSpec((hidden, width), whole),
            pl.BlockSpec((hidden,), lambda r: (0,)),
        ]
        + [pl.BlockSpec((width,), lambda r: (0,))] * 4,
        out_specs=[
            pl.BlockSpec((block, width), cell),
            pl.BlockSpec((width // LANES, block, LANES), lambda r: (0, r, 0)),
            pl.BlockSpec((2, hidden, width), lambda r: (0, 0, 0)),
            pl.BlockSpec((1, hidden), whole),
            pl.BlockSpec((8, width), whole),
        ],
        out_shape=[
            jax.ShapeDtypeStruct((cells, width), BF16),
            jax.ShapeDtypeStruct((width // LANES, cells, LANES), F32),
            jax.ShapeDtypeStruct((2, hidden, width), BF16),
            jax.ShapeDtypeStruct((1, hidden), F32),
            jax.ShapeDtypeStruct((8, width), F32),
        ],
        scratch_shapes=[pltpu.VMEM((2, hidden, width), F32)],
        compiler_params=local_params(),
        name="pointwise",
    )(mixed, state, cot, w_in, w_out, bias_in, *vectors)


def backward_kernel(
    side,
    taps,
    members,
    tiles,
    links_ref,
    grad_ref,
    kern_ref,
    cot_ref,
    state_ref,
    gbin_ref,
    gch_ref,
    big_ref,
    sgrad_ref,
    out_ref,
    sout_ref,
    padded,
    send,
    recv,
    sems,
    core_in,
    x_out,
    x_in,
    t_out,
    t_in,
    own,
    s_pack,
    sm_in,
    st_out,
    st_in,
    s_own,
    core_sem,
    x_sem,
    t_sem,
    g_sem,
    sm_sem,
    st_sem,
    sg_sem,
):
    margin = taps // 2
    parts = padded.shape[0]
    member = lax.axis_index("member")
    tile = lax.axis_index("tile")
    core = lax.rem(member, 2)
    cross = member // 2
    spots = members // 2
    mates = [lax.rem(member + k, members) for k in range(1, members)]
    peers = [lax.rem(tile + k, tiles) for k in range(1, tiles)]
    barrier = pltpu.get_barrier_semaphore()
    for mate in mates:
        pl.semaphore_signal(barrier, inc=1, device_id={"member": mate}, device_id_type=MESH)
    for peer in peers:
        pl.semaphore_signal(barrier, inc=1, device_id={"tile": peer}, device_id_type=MESH)

    def center(part, row):
        at = pl.ds(pl.multiple_of(row * side, side), side)
        return grad_ref[part, at, :].astype(BF16).astype(F32)

    pl.semaphore_wait(barrier, members + tiles - 2)
    pair = [
        remote(
            big_ref.at[kind, :, :, 1 - core], core_in.at[kind], core_sem, kind,
            member=cross * 2 + 1 - core,
        )
        for kind in range(2)
    ]

    place(padded, side, margin, center)
    halo = swap_halo(
        padded, side, margin, links_ref, send, recv, sems, tiles, lambda: None
    )
    lines = s_pack.shape[1]
    s_pack[...] = jnp.zeros_like(s_pack)
    width = s_pack.shape[2]
    first = taps * taps
    extra = gbin_ref.shape[1] // width
    for row in range(extra):
        at = first + row
        s_pack[at // lines, pl.ds(at % lines, 1), :] = gbin_ref[:, pl.ds(row * width, width)]
    for row in range(5):
        at = first + extra + row
        s_pack[at // lines, pl.ds(at % lines, 1), :] = gch_ref[pl.ds(row, 1), :]

    def own_kernel(part):
        def emit(up, col, value):
            at = up * taps + col
            s_pack[at // lines, pl.ds(at % lines, 1), pl.ds(part * LANES, LANES)] = value

        kernel_grad(state_ref, part, grad_ref, side, taps, emit)

    def conv(part):
        lanes = pl.ds(part * LANES, LANES)

        def emit(start, value):
            at = pl.ds(start, side)
            sgrad_ref[at, lanes] = (cot_ref[at, lanes].astype(F32) + value).astype(BF16)

        convolve(padded, part, kern_ref, side, taps, True, emit)

    def cross_over(kind):
        pair[kind].wait()

        def add(t, carry):
            for x in range(spots):
                mine = big_ref[kind, t, x, core].astype(F32)
                x_out[kind, x, t] = (mine + core_in[kind, t, x].astype(F32)).astype(BF16)
            return carry

        lax.fori_loop(0, tiles, add, 0)
        copies = []
        for k in range(1, spots):
            spot = lax.rem(cross + k, spots)
            copies.append(
                remote(
                    x_out.at[kind, spot], x_in.at[kind, k - 1], x_sem, kind * (spots - 1) + k - 1,
                    member=spot * 2 + core,
                )
            )
        return copies

    def go_along(kind, copies):
        for copy in copies:
            copy.wait()

        def add(t, carry):
            value = x_out[kind, cross, t].astype(F32)
            for k in range(spots - 1):
                value = value + x_in[kind, k, t].astype(F32)
            t_out[kind, t] = value.astype(BF16)
            return carry

        lax.fori_loop(0, tiles, add, 0)
        return [
            remote(
                t_out.at[kind, peer], t_in.at[kind, k], t_sem, kind * (tiles - 1) + k, tile=peer
            )
            for k, peer in enumerate(peers)
        ]

    def send_back(kind, copies):
        for copy in copies:
            copy.wait()
        value = t_out[kind, tile].astype(F32)
        for k in range(tiles - 1):
            value = value + t_in[kind, k].astype(F32)
        own[kind] = value.astype(BF16)
        out_ref[kind, member] = value.astype(BF16)
        return [
            remote(
                own.at[kind], out_ref.at[kind, member], g_sem, kind * (members - 1) + k, member=mate
            )
            for k, mate in enumerate(mates)
        ]

    over = [cross_over(0), cross_over(1)]
    for part in range(parts):
        own_kernel(part)
    small = [remote(s_pack, sm_in.at[k], sm_sem, k, member=mate) for k, mate in enumerate(mates)]
    for copy in halo:
        copy.wait()
    take_halo(padded, side, margin, links_ref, recv, tiles)
    conv(0)
    along = [go_along(0, over[0])]
    conv(1)
    along.append(go_along(1, over[1]))
    for copy in small:
        copy.wait()
    total = s_pack[...]
    for k in range(members - 1):
        total = total + sm_in[k]
    st_out[...] = total
    small = [
        remote(st_out.at[peer], st_in.at[k], st_sem, k, tile=peer) for k, peer in enumerate(peers)
    ]
    for part in range(2, parts):
        conv(part)
    back = send_back(0, along[0])
    for copy in small:
        copy.wait()
    total = st_out[tile]
    for k in range(tiles - 1):
        total = total + st_in[k]
    s_own[...] = total
    sout_ref[tile] = total
    small = [
        remote(s_own, sout_ref.at[tile], sg_sem, k, tile=peer) for k, peer in enumerate(peers)
    ]
    back = back + send_back(1, along[1])
    for copy in small + back:
        copy.wait()


def backward_all(links, grad, kern, cot, padded, grad_bin, grad_ch, big, side, members, tiles):
    _, _, spots, _, rows, width = big.shape
    taps = kern.shape[0]
    margin = taps // 2
    used = taps * taps + grad_bin.shape[1] // width + 5
    lines = 8 * (-(-used // (8 * tiles)))
    dma = lambda n: pltpu.SemaphoreType.DMA((2, max(n, 1)))
    return pl.pallas_call(
        functools.partial(backward_kernel, side, taps, members, tiles),
        in_specs=[smem_spec()] + [vmem_spec()] * 7,
        out_specs=[vmem_spec()] * 3,
        out_shape=[
            jax.ShapeDtypeStruct(cot.shape, BF16),
            jax.ShapeDtypeStruct((2, members, rows, width), BF16),
            jax.ShapeDtypeStruct((tiles, lines, width), F32),
        ],
        scratch_shapes=[pltpu.VMEM(padded.shape, F32)]
        + halo_scratch(side, margin, width)
        + [
            pltpu.VMEM((2, tiles, spots, rows, width), BF16),
            pltpu.VMEM((2, spots, tiles, rows, width), BF16),
            pltpu.VMEM((2, max(spots - 1, 1), tiles, rows, width), BF16),
            pltpu.VMEM((2, tiles, rows, width), BF16),
            pltpu.VMEM((2, tiles - 1, rows, width), BF16),
            pltpu.VMEM((2, rows, width), BF16),
            pltpu.VMEM((tiles, lines, width), F32),
            pltpu.VMEM((members - 1, tiles, lines, width), F32),
            pltpu.VMEM((tiles, lines, width), F32),
            pltpu.VMEM((tiles - 1, lines, width), F32),
            pltpu.VMEM((lines, width), F32),
            dma(2),
            dma(2 * (spots - 1)),
            dma(2 * (tiles - 1)),
            dma(2 * (members - 1)),
            dma(members - 1),
            dma(tiles - 1),
            dma(tiles - 1),
        ],
        compiler_params=remote_params(1),
        name="backward_all",
    )(links, grad, kern, cot, padded, grad_bin, grad_ch, big)


def finish_kernel(taps, factor, big_ref, small_ref, win_ref, wout_ref, kern_ref, bin_ref, ch_ref, wide):
    _, members, rows, width = big_ref.shape
    lines = small_ref.shape[1]
    for m in range(members):
        wide[pl.ds(m * rows, rows), :] = big_ref[0, m].astype(F32) * factor
        wout_ref[pl.ds(m * rows, rows), :] = big_ref[1, m].astype(F32) * factor
    win_ref[...] = wide[...].T

    def line(at):
        return small_ref[at // lines, pl.ds(at % lines, 1), :] * factor

    for at in range(taps * taps):
        kern_ref[at // taps, pl.ds(at % taps, 1), :] = line(at)
    first = taps * taps
    extra = bin_ref.shape[0] // width
    for at in range(extra):
        bin_ref[pl.ds(at * width, width)] = line(first + at).reshape(width)
    for at in range(5):
        ch_ref[pl.ds(at, 1), :] = line(first + extra + at)


def finish(big, small, share, taps, hidden, factor):
    width = big.shape[3]
    shapes = [(width, share), (share, width), (taps, taps, width), (hidden,), (5, width)]
    return pl.pallas_call(
        functools.partial(finish_kernel, taps, factor),
        in_specs=[vmem_spec()] * 2,
        out_specs=[vmem_spec()] * 5,
        out_shape=[jax.ShapeDtypeStruct(shape, F32) for shape in shapes],
        scratch_shapes=[pltpu.VMEM((share, width), F32)],
        compiler_params=local_params(),
        name="finish",
    )(big, small)


def body(
    state,
    cotangent,
    neighbors,
    kernel,
    conv_bias,
    norm_gain,
    norm_shift,
    w_in,
    bias_in,
    w_out,
    bias_out,
    layer_scale,
):
    side, width = state.shape[2], state.shape[4]
    cells = side * side
    center = state.reshape(cells, width)
    cot = cotangent.reshape(cells, width)
    hidden = w_in.shape[1]
    taps = kernel.shape[0]
    tiles = lax.axis_size("tile")
    members = lax.axis_size("member")
    mixed, padded = forward_conv(neighbors, center, kernel, conv_bias, side, taps, tiles)
    vectors = (norm_gain, norm_shift, bias_out, layer_scale)
    new_tile, grad_mixed, grad_w, grad_bin, grad_ch = pointwise(
        mixed, center, cot, w_in, w_out, bias_in, vectors
    )
    share = hidden // tiles
    rows = share // members
    big = grad_w.reshape(2, tiles, members // 2, 2, rows, width)
    state_grad, big, small = backward_all(
        neighbors, grad_mixed, kernel, cot, padded, grad_bin, grad_ch, big, side, members, tiles
    )
    factor = 1.0 / math.sqrt(members * tiles * cells)
    shares = finish(big, small, share, taps, hidden, factor)
    return (
        new_tile.reshape(state.shape),
        state_grad.reshape(state.shape),
        *shares,
    )


def solution(mesh):
    tiled = P("member", "tile", None, None, None)
    in_specs = (tiled, tiled) + (P(),) * 10
    out_specs = (tiled, tiled, P(None, "tile"), P("tile", None), P(), P(), P())
    return jax.shard_map(body, mesh=mesh, in_specs=in_specs, out_specs=out_specs, check_vma=False)
```

```python
import functools
import math

import jax
import jax.numpy as jnp
from jax import lax
from jax.experimental import pallas as pl
from jax.experimental.pallas import tpu as pltpu
from jax.sharding import PartitionSpec as P

OFFSETS = (1, 2, 3, -1, -2, -3)
GELU_SCALE = 0.7978845608028654
GELU_CUBIC = 0.044715
EPSILON = 1e-06
LANES = 128
LEAD = 8
MESH = pl.DeviceIdType.MESH
F32 = jnp.float32
BF16 = jnp.bfloat16
VMEM_LIMIT = 56 << 20


def vmem_spec():
    return pl.BlockSpec(memory_space=pltpu.VMEM)


def smem_spec():
    return pl.BlockSpec(memory_space=pltpu.SMEM)


def local_params():
    return pltpu.CompilerParams(vmem_limit_bytes=VMEM_LIMIT)


def remote_params(ident):
    return pltpu.CompilerParams(
        collective_id=ident, has_side_effects=True, vmem_limit_bytes=VMEM_LIMIT
    )


def pitch_of(side):
    return side + 2 * LEAD


def spread_of(side, margin):
    return (side + 2 * margin) * pitch_of(side)


def place(padded, side, margin, center):
    pitch = pitch_of(side)
    for part in range(padded.shape[0]):

        def clear(row, carry):
            at = pl.ds(pl.multiple_of(row * pitch, 8), pitch)
            padded[part, at, :] = jnp.zeros((pitch, LANES), F32)
            return carry

        lax.fori_loop(0, side + 2 * margin, clear, 0)

        def put(row, carry):
            at = pl.ds(pl.multiple_of((margin + row) * pitch + LEAD, 8), side)
            padded[part, at, :] = center(part, row)
            return carry

        lax.fori_loop(0, side, put, 0)


def around(tile, count):
    takers = [lax.rem(tile + offset + count, count) for offset in OFFSETS]
    givers = [lax.rem(tile - offset + count, count) for offset in OFFSETS]
    return takers, givers


def pack(padded, side, margin, want, send_ref):
    pitch = pitch_of(side)
    edge = side - margin
    for part in range(padded.shape[0]):
        lanes = pl.ds(part * LANES, LANES)
        for k in range(margin):
            low = (margin + k) * pitch + LEAD
            high = (margin + edge + k) * pitch + LEAD
            first = margin * pitch + LEAD
            lines = [
                padded[part, pl.ds(low, side), :],
                padded[part, pl.ds(high, side), :],
                padded[part, pl.ds(first + k, side, stride=pitch), :],
                padded[part, pl.ds(first + edge + k, side, stride=pitch), :],
            ]
            lines = lines + [
                jnp.concatenate([lines[0][:8]] * (side // 8), axis=0),
                jnp.concatenate([lines[0][side - 8 :]] * (side // 8), axis=0),
                jnp.concatenate([lines[1][:8]] * (side // 8), axis=0),
                jnp.concatenate([lines[1][side - 8 :]] * (side // 8), axis=0),
            ]
            for slot in range(len(OFFSETS)):
                line = lines[7]
                for way in range(7):
                    line = jnp.where(want[slot][way], lines[way], line)
                send_ref[slot, k, :, lanes] = line.astype(BF16)


def unpack(padded, side, margin, have, recv_ref):
    pitch = pitch_of(side)
    for part in range(padded.shape[0]):
        lanes = pl.ds(part * LANES, LANES)
        for k in range(margin):
            lines = [recv_ref[slot, k, :, lanes].astype(F32) for slot in range(len(OFFSETS))]
            for way in range(8):
                size = side if way < 4 else 8
                line = jnp.zeros((size, LANES), F32)
                for slot in range(len(OFFSETS)):
                    line = jnp.where(have[slot][way], lines[slot][:size], line)
                if way == 0:
                    at = pl.ds((margin + side + k) * pitch + LEAD, side)
                elif way == 1:
                    at = pl.ds(k * pitch + LEAD, side)
                elif way == 2:
                    at = pl.ds(margin * pitch + LEAD + side + k, side, stride=pitch)
                elif way == 3:
                    at = pl.ds(margin * pitch + LEAD - margin + k, side, stride=pitch)
                else:
                    row = margin + side + k if way in (4, 5) else k
                    at = pl.ds(row * pitch + (LEAD + side if way in (4, 6) else LEAD - 8), 8)
                padded[part, at, :] = line


def convolve(padded, part, kern_ref, side, taps, flipped, emit, group=4, first=0, gap=1, steps=None):
    pitch = pitch_of(side)
    margin = taps // 2
    lanes = pl.ds(part * LANES, LANES)

    def step(index, carry):
        base = (first + index * gap) * group
        total = [jnp.zeros((side, LANES), F32) for _ in range(group)]
        for col in range(taps):
            for row in range(group + taps - 1):
                start = (base + row) * pitch
                line = padded[part, pl.ds(start + (LEAD - margin + col), side), :]
                for out in range(group):
                    up = row - out
                    if 0 <= up < taps:
                        a, b = (taps - 1 - up, taps - 1 - col) if flipped else (up, col)
                        total[out] = total[out] + kern_ref[a, pl.ds(b, 1), lanes] * line
        for out in range(group):
            emit(pl.multiple_of((base + out) * side, side), total[out])
        return carry

    lax.fori_loop(0, side // group if steps is None else steps, step, 0)


def edge_columns(sides, part, kern_ref, side, taps, add, group=4):
    margin = taps // 2
    lanes = pl.ds(part * LANES, LANES)

    def step(index, carry):
        base = (1 + index) * group
        for east in range(2):
            total = [jnp.zeros((8, LANES), F32) for _ in range(group)]
            for near in range(margin):
                col = margin + 1 + near if east else near
                shift = 1 + near if east else 8 - margin + near
                for row in range(group + taps - 1):
                    line = sides[east, part, pl.ds((base + row) * 16 + shift, 8), :]
                    for out in range(group):
                        up = row - out
                        if 0 <= up < taps:
                            total[out] = total[out] + kern_ref[up, pl.ds(col, 1), lanes] * line
            for out in range(group):
                start = (base + out) * side + (side - 8 if east else 0)
                add(pl.multiple_of(start, 8), total[out])
        return carry

    lax.fori_loop(0, side // group - 2, step, 0)


def kernel_grad(padded, part, grad_ref, side, taps, emit, group=4):
    pitch = pitch_of(side)
    margin = taps // 2
    for col in range(taps):

        def step(index, sums):
            sums = list(sums)
            base = index * group
            grads = [
                grad_ref[part, pl.ds(pl.multiple_of((base + out) * side, side), side), :]
                for out in range(group)
            ]
            for row in range(group + taps - 1):
                start = (base + row) * pitch
                line = padded[part, pl.ds(start + (LEAD - margin + col), side), :]
                for out in range(group):
                    up = row - out
                    if 0 <= up < taps:
                        product = line * grads[out]
                        for piece in range(side // 8):
                            sums[up] = sums[up] + product[piece * 8 : piece * 8 + 8]
            return tuple(sums)

        zero = jnp.zeros((8, LANES), F32)
        sums = lax.fori_loop(0, side // group, step, (zero,) * taps)
        for up in range(taps):
            emit(up, col, jnp.sum(sums[up], axis=0, keepdims=True))


def remote(source, target, sems, slot, **device):
    copy = pltpu.make_async_remote_copy(
        src_ref=source,
        dst_ref=target,
        send_sem=sems.at[0, slot],
        recv_sem=sems.at[1, slot],
        device_id=device,
        device_id_type=MESH,
    )
    copy.start()
    return copy


def swap_halo(padded, side, margin, links_ref, send_ref, recv_ref, sems, count, ready):
    tile = lax.axis_index("tile")
    takers, _ = around(tile, count)
    want = [[links_ref[taker, way] == tile for way in range(8)] for taker in takers]
    pack(padded, side, margin, want, send_ref)
    ready()
    return [
        remote(send_ref.at[slot], recv_ref.at[slot], sems, slot, tile=taker)
        for slot, taker in enumerate(takers)
    ]


def take_halo(padded, side, margin, links_ref, recv_ref, count):
    tile = lax.axis_index("tile")
    _, givers = around(tile, count)
    have = [[links_ref[tile, way] == giver for way in range(8)] for giver in givers]
    unpack(padded, side, margin, have, recv_ref)


def forward_kernel(
    side, taps, count, links_ref, tile_ref, kern_ref, bias_ref, mixed_ref, padded, send, recv, sems, sides
):
    margin = taps // 2
    barrier = pltpu.get_barrier_semaphore()
    takers, _ = around(lax.axis_index("tile"), count)
    for taker in takers:
        pl.semaphore_signal(barrier, inc=1, device_id={"tile": taker}, device_id_type=MESH)

    def center(part, row):
        at = pl.ds(pl.multiple_of(row * side, side), side)
        return tile_ref[at, pl.ds(part * LANES, LANES)].astype(F32)

    place(padded, side, margin, center)
    copies = swap_halo(
        padded, side, margin, links_ref, send, recv, sems, count,
        lambda: pl.semaphore_wait(barrier, len(OFFSETS)),
    )
    parts = padded.shape[0]
    groups = side // 4
    pitch = pitch_of(side)

    def make_emit(part):
        lanes = pl.ds(part * LANES, LANES)
        bias = bias_ref[lanes].reshape(1, LANES)

        def emit(start, value):
            mixed_ref[pl.ds(start, side), lanes] = value + bias

        return emit

    for part in range(parts):
        convolve(
            padded, part, kern_ref, side, taps, False, make_emit(part), first=1, steps=groups - 2
        )
    for copy in copies:
        copy.wait()
    take_halo(padded, side, margin, links_ref, recv, count)
    for part in range(parts):
        lanes = pl.ds(part * LANES, LANES)

        def frame(row, carry):
            at = pl.ds(pl.multiple_of(row * 16, 8), 8)
            after = pl.ds(pl.multiple_of(row * 16 + 8, 8), 8)
            start = row * pitch + LEAD
            blank = jnp.zeros((8, LANES), F32)
            sides[0, part, at, :] = padded[part, pl.ds(pl.multiple_of(start - 8, 8), 8), :]
            sides[0, part, after, :] = blank
            sides[1, part, at, :] = blank
            sides[1, part, after, :] = padded[part, pl.ds(pl.multiple_of(start + side, 8), 8), :]
            return carry

        lax.fori_loop(0, side + 2 * margin, frame, 0)

        def add(start, value):
            mixed_ref[pl.ds(start, 8), lanes] += value

        convolve(
            padded, part, kern_ref, side, taps, False, make_emit(part), gap=groups - 1, steps=2
        )
        edge_columns(sides, part, kern_ref, side, taps, add)


def halo_scratch(side, margin, width):
    pieces = (len(OFFSETS), margin, side, width)
    return [
        pltpu.VMEM(pieces, BF16),
        pltpu.VMEM(pieces, BF16),
        pltpu.SemaphoreType.DMA((2, len(OFFSETS))),
    ]


def forward_conv(links, tile, kern, bias, side, taps, count):
    cells, width = tile.shape
    margin = taps // 2
    return pl.pallas_call(
        functools.partial(forward_kernel, side, taps, count),
        in_specs=[smem_spec()] + [vmem_spec()] * 3,
        out_specs=[vmem_spec()] * 2,
        out_shape=[
            jax.ShapeDtypeStruct((cells, width), F32),
            jax.ShapeDtypeStruct((width // LANES, spread_of(side, margin), LANES), F32),
        ],
        scratch_shapes=halo_scratch(side, margin, width)
        + [pltpu.VMEM((2, width // LANES, (side + 2 * margin) * 16, LANES), F32)],
        compiler_params=remote_params(0),
        name="forward_conv",
    )(links, tile, kern, bias)


def contract_rows(left, right):
    return lax.dot_general(left, right, (((0,), (0,)), ((), ())), preferred_element_type=F32)


def contract_cols(left, right):
    return lax.dot_general(left, right, (((1,), (1,)), ((), ())), preferred_element_type=F32)


def mlp_kernel(
    chunk,
    mixed_ref,
    state_ref,
    cot_ref,
    win_ref,
    wout_ref,
    bin_ref,
    gain_ref,
    shift_ref,
    bout_ref,
    scale_ref,
    new_ref,
    gmix_ref,
    gw_ref,
    gbin_ref,
    gch_ref,
    acc_ref,
):
    step = pl.program_id(0)
    last = pl.num_programs(0) - 1
    hidden = win_ref.shape[1]
    gain, shift, bout, scale = (
        ref[...].reshape(1, -1) for ref in (gain_ref, shift_ref, bout_ref, scale_ref)
    )

    @pl.when(step == 0)
    def _():
        acc_ref[...] = jnp.zeros_like(acc_ref)
        gbin_ref[...] = jnp.zeros_like(gbin_ref)
        gch_ref[...] = jnp.zeros_like(gch_ref)

    mixed = mixed_ref[...]
    centered = mixed - jnp.mean(mixed, axis=1, keepdims=True)
    variance = jnp.mean(centered * centered, axis=1, keepdims=True)
    inv_std = lax.rsqrt(variance + EPSILON)
    norm_hat = centered * inv_std
    normed = (norm_hat * gain + shift).astype(BF16)
    cot = cot_ref[...].astype(F32)
    grad_branch = scale * cot
    branch_low = grad_branch.astype(BF16)

    branch = jnp.zeros_like(mixed)
    grad_normed = jnp.zeros_like(mixed)
    for at in range(0, hidden, chunk):
        win = win_ref[:, at : at + chunk]
        wout = wout_ref[at : at + chunk, :]
        pre = jnp.dot(normed, win, preferred_element_type=F32) + bin_ref[pl.ds(at, chunk)].reshape(1, chunk)
        square = pre * pre
        tanh_value = jnp.tanh(GELU_SCALE * pre * (1.0 + GELU_CUBIC * square))
        half = 0.5 * (1.0 + tanh_value)
        activation = (pre * half).astype(BF16)
        slope = half + (0.5 * GELU_SCALE) * pre * (1.0 - tanh_value * tanh_value) * (
            1.0 + 3.0 * GELU_CUBIC * square
        )
        grad_pre = contract_cols(branch_low, wout) * slope
        grad_low = grad_pre.astype(BF16)
        branch = branch + jnp.dot(activation, wout, preferred_element_type=F32)
        grad_normed = grad_normed + contract_cols(grad_low, win)
        acc_ref[0, at : at + chunk, :] += contract_rows(grad_low, normed)
        acc_ref[1, at : at + chunk, :] += contract_rows(activation, branch_low)
        gbin_ref[:, at : at + chunk] += jnp.sum(grad_pre, axis=0, keepdims=True)

    branch = branch + bout
    new_ref[...] = (state_ref[...].astype(F32) + scale * branch).astype(BF16)
    scaled = grad_normed * gain
    grad_mixed = inv_std * (
        scaled
        - jnp.mean(scaled, axis=1, keepdims=True)
        - norm_hat * jnp.mean(scaled * norm_hat, axis=1, keepdims=True)
    )
    for part in range(gmix_ref.shape[0]):
        gmix_ref[part] = grad_mixed[:, part * LANES : (part + 1) * LANES]
    gch_ref[0:1, :] += jnp.sum(grad_mixed, axis=0, keepdims=True)
    gch_ref[1:2, :] += jnp.sum(grad_normed * norm_hat, axis=0, keepdims=True)
    gch_ref[2:3, :] += jnp.sum(grad_normed, axis=0, keepdims=True)
    gch_ref[3:4, :] += jnp.sum(grad_branch, axis=0, keepdims=True)
    gch_ref[4:5, :] += jnp.sum(cot * branch, axis=0, keepdims=True)

    @pl.when(step == last)
    def _():
        gw_ref[...] = acc_ref[...].astype(BF16)


def pointwise(mixed, state, cot, w_in, w_out, bias_in, vectors, block=512, chunk=768):
    cells, width = mixed.shape
    hidden = w_in.shape[1]
    cell = lambda r: (r, 0)
    whole = lambda r: (0, 0)
    return pl.pallas_call(
        functools.partial(mlp_kernel, chunk),
        grid=(cells // block,),
        in_specs=[
            pl.BlockSpec((block, width), cell),
            pl.BlockSpec((block, width), cell),
            pl.BlockSpec((block, width), cell),
            pl.BlockSpec((width, hidden), whole),
            pl.BlockSpec((hidden, width), whole),
            pl.BlockSpec((hidden,), lambda r: (0,)),
        ]
        + [pl.BlockSpec((width,), lambda r: (0,))] * 4,
        out_specs=[
            pl.BlockSpec((block, width), cell),
            pl.BlockSpec((width // LANES, block, LANES), lambda r: (0, r, 0)),
            pl.BlockSpec((2, hidden, width), lambda r: (0, 0, 0)),
            pl.BlockSpec((1, hidden), whole),
            pl.BlockSpec((8, width), whole),
        ],
        out_shape=[
            jax.ShapeDtypeStruct((cells, width), BF16),
            jax.ShapeDtypeStruct((width // LANES, cells, LANES), F32),
            jax.ShapeDtypeStruct((2, hidden, width), BF16),
            jax.ShapeDtypeStruct((1, hidden), F32),
            jax.ShapeDtypeStruct((8, width), F32),
        ],
        scratch_shapes=[pltpu.VMEM((2, hidden, width), F32)],
        compiler_params=local_params(),
        name="pointwise",
    )(mixed, state, cot, w_in, w_out, bias_in, *vectors)


def backward_kernel(
    side,
    taps,
    members,
    tiles,
    links_ref,
    grad_ref,
    kern_ref,
    cot_ref,
    state_ref,
    gbin_ref,
    gch_ref,
    big_ref,
    sgrad_ref,
    out_ref,
    sout_ref,
    padded,
    send,
    recv,
    sems,
    core_in,
    x_out,
    x_in,
    t_out,
    t_in,
    own,
    s_pack,
    sm_in,
    st_out,
    st_in,
    s_own,
    core_sem,
    x_sem,
    t_sem,
    g_sem,
    sm_sem,
    st_sem,
    sg_sem,
):
    margin = taps // 2
    parts = padded.shape[0]
    member = lax.axis_index("member")
    tile = lax.axis_index("tile")
    core = lax.rem(member, 2)
    cross = member // 2
    spots = members // 2
    mates = [lax.rem(member + k, members) for k in range(1, members)]
    peers = [lax.rem(tile + k, tiles) for k in range(1, tiles)]
    barrier = pltpu.get_barrier_semaphore()
    for mate in mates:
        pl.semaphore_signal(barrier, inc=1, device_id={"member": mate}, device_id_type=MESH)
    for peer in peers:
        pl.semaphore_signal(barrier, inc=1, device_id={"tile": peer}, device_id_type=MESH)

    def center(part, row):
        at = pl.ds(pl.multiple_of(row * side, side), side)
        return grad_ref[part, at, :].astype(BF16).astype(F32)

    pl.semaphore_wait(barrier, members + tiles - 2)
    pair = [
        remote(
            big_ref.at[kind, :, :, 1 - core], core_in.at[kind], core_sem, kind,
            member=cross * 2 + 1 - core,
        )
        for kind in range(2)
    ]

    place(padded, side, margin, center)
    halo = swap_halo(
        padded, side, margin, links_ref, send, recv, sems, tiles, lambda: None
    )
    lines = s_pack.shape[1]
    s_pack[...] = jnp.zeros_like(s_pack)
    width = s_pack.shape[2]
    first = taps * taps
    extra = gbin_ref.shape[1] // width
    for row in range(extra):
        at = first + row
        s_pack[at // lines, pl.ds(at % lines, 1), :] = gbin_ref[:, pl.ds(row * width, width)]
    for row in range(5):
        at = first + extra + row
        s_pack[at // lines, pl.ds(at % lines, 1), :] = gch_ref[pl.ds(row, 1), :]

    def own_kernel(part):
        def emit(up, col, value):
            at = up * taps + col
            s_pack[at // lines, pl.ds(at % lines, 1), pl.ds(part * LANES, LANES)] = value

        kernel_grad(state_ref, part, grad_ref, side, taps, emit)

    def conv(part):
        lanes = pl.ds(part * LANES, LANES)

        def emit(start, value):
            at = pl.ds(start, side)
            sgrad_ref[at, lanes] = (cot_ref[at, lanes].astype(F32) + value).astype(BF16)

        convolve(padded, part, kern_ref, side, taps, True, emit)

    def cross_over(kind):
        pair[kind].wait()

        def add(t, carry):
            for x in range(spots):
                mine = big_ref[kind, t, x, core].astype(F32)
                x_out[kind, x, t] = (mine + core_in[kind, t, x].astype(F32)).astype(BF16)
            return carry

        lax.fori_loop(0, tiles, add, 0)
        copies = []
        for k in range(1, spots):
            spot = lax.rem(cross + k, spots)
            copies.append(
                remote(
                    x_out.at[kind, spot], x_in.at[kind, k - 1], x_sem, kind * (spots - 1) + k - 1,
                    member=spot * 2 + core,
                )
            )
        return copies

    def go_along(kind, copies):
        for copy in copies:
            copy.wait()

        def add(t, carry):
            value = x_out[kind, cross, t].astype(F32)
            for k in range(spots - 1):
                value = value + x_in[kind, k, t].astype(F32)
            t_out[kind, t] = value.astype(BF16)
            return carry

        lax.fori_loop(0, tiles, add, 0)
        return [
            remote(
                t_out.at[kind, peer], t_in.at[kind, k], t_sem, kind * (tiles - 1) + k, tile=peer
            )
            for k, peer in enumerate(peers)
        ]

    def send_back(kind, copies):
        for copy in copies:
            copy.wait()
        value = t_out[kind, tile].astype(F32)
        for k in range(tiles - 1):
            value = value + t_in[kind, k].astype(F32)
        own[kind] = value.astype(BF16)
        out_ref[kind, member] = value.astype(BF16)
        return [
            remote(
                own.at[kind], out_ref.at[kind, member], g_sem, kind * (members - 1) + k, member=mate
            )
            for k, mate in enumerate(mates)
        ]

    own_kernel(0)
    over = [cross_over(0)]
    own_kernel(1)
    over.append(cross_over(1))
    for part in range(2, parts):
        own_kernel(part)
    small = [remote(s_pack, sm_in.at[k], sm_sem, k, member=mate) for k, mate in enumerate(mates)]
    for copy in halo:
        copy.wait()
    take_halo(padded, side, margin, links_ref, recv, tiles)
    conv(0)
    along = [go_along(0, over[0])]
    conv(1)
    along.append(go_along(1, over[1]))
    for copy in small:
        copy.wait()
    total = s_pack[...]
    for k in range(members - 1):
        total = total + sm_in[k]
    st_out[...] = total
    small = [
        remote(st_out.at[peer], st_in.at[k], st_sem, k, tile=peer) for k, peer in enumerate(peers)
    ]
    for part in range(2, parts):
        conv(part)
    back = send_back(0, along[0])
    for copy in small:
        copy.wait()
    total = st_out[tile]
    for k in range(tiles - 1):
        total = total + st_in[k]
    s_own[...] = total
    sout_ref[tile] = total
    small = [
        remote(s_own, sout_ref.at[tile], sg_sem, k, tile=peer) for k, peer in enumerate(peers)
    ]
    back = back + send_back(1, along[1])
    for copy in small + back:
        copy.wait()


def backward_all(links, grad, kern, cot, padded, grad_bin, grad_ch, big, side, members, tiles):
    _, _, spots, _, rows, width = big.shape
    taps = kern.shape[0]
    margin = taps // 2
    used = taps * taps + grad_bin.shape[1] // width + 5
    lines = 8 * (-(-used // (8 * tiles)))
    dma = lambda n: pltpu.SemaphoreType.DMA((2, max(n, 1)))
    return pl.pallas_call(
        functools.partial(backward_kernel, side, taps, members, tiles),
        in_specs=[smem_spec()] + [vmem_spec()] * 7,
        out_specs=[vmem_spec()] * 3,
        out_shape=[
            jax.ShapeDtypeStruct(cot.shape, BF16),
            jax.ShapeDtypeStruct((2, members, rows, width), BF16),
            jax.ShapeDtypeStruct((tiles, lines, width), F32),
        ],
        scratch_shapes=[pltpu.VMEM(padded.shape, F32)]
        + halo_scratch(side, margin, width)
        + [
            pltpu.VMEM((2, tiles, spots, rows, width), BF16),
            pltpu.VMEM((2, spots, tiles, rows, width), BF16),
            pltpu.VMEM((2, max(spots - 1, 1), tiles, rows, width), BF16),
            pltpu.VMEM((2, tiles, rows, width), BF16),
            pltpu.VMEM((2, tiles - 1, rows, width), BF16),
            pltpu.VMEM((2, rows, width), BF16),
            pltpu.VMEM((tiles, lines, width), F32),
            pltpu.VMEM((members - 1, tiles, lines, width), F32),
            pltpu.VMEM((tiles, lines, width), F32),
            pltpu.VMEM((tiles - 1, lines, width), F32),
            pltpu.VMEM((lines, width), F32),
            dma(2),
            dma(2 * (spots - 1)),
            dma(2 * (tiles - 1)),
            dma(2 * (members - 1)),
            dma(members - 1),
            dma(tiles - 1),
            dma(tiles - 1),
        ],
        compiler_params=remote_params(1),
        name="backward_all",
    )(links, grad, kern, cot, padded, grad_bin, grad_ch, big)


def finish_kernel(taps, factor, big_ref, small_ref, win_ref, wout_ref, kern_ref, bin_ref, ch_ref):
    _, members, rows, width = big_ref.shape
    lines = small_ref.shape[1]
    for m in range(members):
        win_ref[pl.ds(m * rows, rows), :] = big_ref[0, m].astype(F32) * factor
        wout_ref[pl.ds(m * rows, rows), :] = big_ref[1, m].astype(F32) * factor

    def line(at):
        return small_ref[at // lines, pl.ds(at % lines, 1), :] * factor

    for at in range(taps * taps):
        kern_ref[at // taps, pl.ds(at % taps, 1), :] = line(at)
    first = taps * taps
    extra = bin_ref.shape[0] // width
    for at in range(extra):
        bin_ref[pl.ds(at * width, width)] = line(first + at).reshape(width)
    for at in range(5):
        ch_ref[pl.ds(at, 1), :] = line(first + extra + at)


def finish(big, small, share, taps, hidden, factor):
    width = big.shape[3]
    shapes = [(share, width), (share, width), (taps, taps, width), (hidden,), (5, width)]
    return pl.pallas_call(
        functools.partial(finish_kernel, taps, factor),
        in_specs=[vmem_spec()] * 2,
        out_specs=[vmem_spec()] * 5,
        out_shape=[jax.ShapeDtypeStruct(shape, F32) for shape in shapes],
        compiler_params=local_params(),
        name="finish",
    )(big, small)


def body(
    state,
    cotangent,
    neighbors,
    kernel,
    conv_bias,
    norm_gain,
    norm_shift,
    w_in,
    bias_in,
    w_out,
    bias_out,
    layer_scale,
):
    side, width = state.shape[2], state.shape[4]
    cells = side * side
    center = state.reshape(cells, width)
    cot = cotangent.reshape(cells, width)
    hidden = w_in.shape[1]
    taps = kernel.shape[0]
    tiles = lax.axis_size("tile")
    members = lax.axis_size("member")
    mixed, padded = forward_conv(neighbors, center, kernel, conv_bias, side, taps, tiles)
    vectors = (norm_gain, norm_shift, bias_out, layer_scale)
    new_tile, grad_mixed, grad_w, grad_bin, grad_ch = pointwise(
        mixed, center, cot, w_in, w_out, bias_in, vectors
    )
    share = hidden // tiles
    rows = share // members
    big = grad_w.reshape(2, tiles, members // 2, 2, rows, width)
    state_grad, big, small = backward_all(
        neighbors, grad_mixed, kernel, cot, padded, grad_bin, grad_ch, big, side, members, tiles
    )
    factor = 1.0 / math.sqrt(members * tiles * cells)
    win_share, *shares = finish(big, small, share, taps, hidden, factor)
    return (
        new_tile.reshape(state.shape),
        state_grad.reshape(state.shape),
        win_share.T,
        *shares,
    )


def solution(mesh):
    tiled = P("member", "tile", None, None, None)
    in_specs = (tiled, tiled) + (P(),) * 10
    out_specs = (tiled, tiled, P(None, "tile"), P("tile", None), P(), P(), P())
    return jax.shard_map(body, mesh=mesh, in_specs=in_specs, out_specs=out_specs, check_vma=False)
```
